256 devices in a mesh: ia: 4 (over y), ja: 4 (over x), ka: 16 (over z, core).
Axes of the slice: x: 4, y: 4, z: 8, core: 2. Of those that a mesh axis runs over, the one named last changes fastest.
Arguments:
- blocks: bfloat16 [4, 4, 16, 2, 128, 128, 128], P('ia', 'ja', 'ka'), may hold values from -6 to 6
- first_mode_rows: int32 [4, 4, 16, 2], P('ia', 'ja', 'ka'), may hold values from 0 to 15
- second_mode_rows: int32 [4, 4, 16, 2], P('ia', 'ja', 'ka'), may hold values from 0 to 15
- third_mode_rows: int32 [4, 4, 16, 2], P('ia', 'ja', 'ka'), may hold values from 0 to 3
- filled: int32 [4, 4, 16], P('ia', 'ja', 'ka'), may hold values from 1 to 2, as said below
- owner_one: int32 [64], replicated, may hold values from 0 to 63, each once
- owner_two: int32 [64], replicated, may hold values from 0 to 63, each once
- factor_b: float32 [4, 2048, 256], P('ja', ('ia', 'ka'))
- factor_c: float32 [16, 512, 256], P('ka')
Outputs:
- a_new: float32 [4, 2048, 256], P('ia', ('ja', 'ka'))
- b_new: float32 [4, 2048, 256], P('ja', ('ia', 'ka'))
The draws below stay inside these ranges and needn't reach their ends.
Inputs may be any that keep to these rules, and one draw needn't show every extreme that they name: Number of nonempty slots of a grid cell; at least one cell has all 2 slots filled. Slots at or beyond this count hold data that is not part of the tensor.
All inputs are finite; a program needn't handle non-finite values.
Results may differ from the reference program's by a relative error of at most 0.0039.
The reference program's roundings to bfloat16 on the way count: a program that leaves them out, or rounds other values in their place, can miss the bound.
Values may be sent and summed in bfloat16 or wider, within the bound.
A program may use at most 128 MiB of HBM per device.

```python
import math
import jax
import jax.numpy as jnp
from jax import lax

R = 256
BLOCK_SIDE = 128
SLOTS_PER_CARD = 2
SLAB_TWO = 2048
SLAB_THREE = 512
SLAB_BLOCKS_ONE = 16
SLAB_BLOCKS_TWO = 16
SLAB_BLOCKS_THREE = 4
PIECES_ONE = 64
PIECES_TWO = 64
ROWS_TWO = 8192
ROWS_THREE = 8192
N_IA = 4
N_JA = 4
N_KA = 16


CORRELATION = 0.92


def factor_law(key, leading, slab_rows, rank_width, total_rows, column_order):
    keys = jax.random.split(key, 3)
    taps_count = 32
    padded_width = rank_width + taps_count - 1
    place = jnp.arange(leading, dtype=jnp.float32)[:, None] * slab_rows + jnp.arange(slab_rows, dtype=jnp.float32)[None, :]
    rising = 1.0 + 2.0 * place / max(leading * slab_rows - 1, 1)
    raw_noise = jax.random.normal(keys[0], (leading, slab_rows, padded_width), jnp.float32)
    common = 0.7
    spread = math.log(10.0)
    filtered = raw_noise
    stride = 1
    for level_index in range(5):
        filtered = filtered[..., stride:] + CORRELATION ** stride * filtered[..., :-stride]
        stride = stride * 2
    norm_square = (1.0 - CORRELATION ** (2 * taps_count)) / (1.0 - CORRELATION ** 2)
    filtered = filtered / math.sqrt(norm_square)
    filtered = filtered[..., column_order]
    shared = jax.random.normal(keys[1], (leading, slab_rows, 1), jnp.float32)
    row_scale = jnp.exp(jax.random.uniform(keys[2], (leading, slab_rows, 1), jnp.float32) * spread)
    base = 0.2 * math.sqrt(BLOCK_SIDE) / total_rows
    return base * rising[..., None] * row_scale * (filtered + common * shared)


def rank_order(key):
    return jax.random.permutation(jax.random.fold_in(key, 99), R)


def draw_factor_b(key, part):
    return factor_law(jax.random.fold_in(key, 1), N_JA, SLAB_TWO, R, ROWS_TWO, rank_order(key))


def draw_factor_c(key, part):
    return factor_law(jax.random.fold_in(key, 2), N_KA, SLAB_THREE, R, ROWS_THREE, rank_order(key))


def draw_filled(key, part):
    unscaled_counts = jax.random.randint(key, (N_IA, N_JA, N_KA), 0, 7)
    count_values = jnp.minimum(1 + jnp.maximum(unscaled_counts - 4, 0), SLOTS_PER_CARD)
    return count_values.at[0, 0, 0].set(SLOTS_PER_CARD).astype(jnp.int32)


def place_ends(drawn, own_key, low, high):
    index_at = [jax.random.randint(jax.random.fold_in(own_key, axis), (), 0, length) for axis, length in enumerate(drawn.shape)]
    widest = drawn.shape.index(max(drawn.shape))
    next_to = index_at[:widest] + [(index_at[widest] + 1) % drawn.shape[widest]] + index_at[widest + 1:]
    return drawn.at[tuple(index_at)].set(low).at[tuple(next_to)].set(high)


def steps_of(stream_key, extent, pieces, least, top_value):
    factor_of = 1.0
    for dim, parts in pieces:
        heights = jax.random.uniform(jax.random.fold_in(jax.random.fold_in(stream_key, 6), dim), (parts,), jnp.float32, least / len(pieces), top_value / len(pieces))
        factor_of = factor_of * jnp.repeat(jnp.exp(heights), extent[dim] // parts).reshape((-1,) + (1,) * (len(extent) - 1 - dim))
    return factor_of


def scatter_about(stream_key, extent, deviation, bound, pieces=(), kind=jnp.bfloat16):
    array = jax.random.normal(stream_key, extent, jnp.float32) * deviation
    if len(pieces) > 0:
        array = steps_of(stream_key, extent, pieces, -0.22, 0.18) * array
    return jnp.clip(array, min=-bound, max=bound).astype(kind)


def setup_inputs(seed: int = 0) -> dict:
    arg_keys = jax.random.split(jax.random.key(seed), 10)
    return {
        "blocks": scatter_about(arg_keys[0], (N_IA, N_JA, N_KA, SLOTS_PER_CARD, BLOCK_SIDE, BLOCK_SIDE, BLOCK_SIDE), 1.0, 6.0, ((0, 4), (1, 4), (2, 16))),
        "first_mode_rows": place_ends(jax.random.randint(arg_keys[1], (N_IA, N_JA, N_KA, SLOTS_PER_CARD), 0, SLAB_BLOCKS_ONE), jax.random.fold_in(arg_keys[1], 1), 0, SLAB_BLOCKS_ONE - 1).astype(jnp.int32),
        "second_mode_rows": place_ends(jax.random.randint(arg_keys[2], (N_IA, N_JA, N_KA, SLOTS_PER_CARD), 0, SLAB_BLOCKS_TWO), jax.random.fold_in(arg_keys[2], 1), 0, SLAB_BLOCKS_TWO - 1).astype(jnp.int32),
        "third_mode_rows": place_ends(jax.random.randint(arg_keys[3], (N_IA, N_JA, N_KA, SLOTS_PER_CARD), 0, SLAB_BLOCKS_THREE), jax.random.fold_in(arg_keys[3], 1), 0, SLAB_BLOCKS_THREE - 1).astype(jnp.int32),
        "filled": draw_filled(jax.random.fold_in(arg_keys[9], 71), 0),
        "owner_one": jax.random.permutation(arg_keys[5], PIECES_ONE).astype(jnp.int32),
        "owner_two": jax.random.permutation(arg_keys[6], PIECES_TWO).astype(jnp.int32),
        "factor_b": draw_factor_b(jax.random.fold_in(arg_keys[9], 71), 0),
        "factor_c": draw_factor_c(jax.random.fold_in(arg_keys[9], 71), 0),
    }


EPS = 1e-06

def solve_rows(gram, rows):
    lower = jnp.linalg.cholesky(gram)
    return jax.scipy.linalg.cho_solve((lower, True), rows.T).T

def add_rows(accum, start, contrib):
    current = lax.dynamic_slice_in_dim(accum, start, contrib.shape[0], 0)
    return lax.dynamic_update_slice_in_dim(accum, current + contrib, start, 0)

def batched_sum(inner, weights):
    summed = lax.dot_general(inner.astype(jnp.float32), weights.astype(jnp.float32), (((1,), (0,)), ((2,), (1,))), precision=lax.Precision.HIGHEST, preferred_element_type=jnp.float32)
    return summed.T

def reference(blocks, first_mode_rows, second_mode_rows, third_mode_rows, filled, owner_one, owner_two, factor_b, factor_c):
    highest = lax.Precision.HIGHEST
    grid_i, grid_j, grid_k, slot_count = blocks.shape[:4]
    block_edge = blocks.shape[-1]
    rank_width = factor_b.shape[2]
    pieces_two = owner_two.shape[0]
    pieces_one = owner_one.shape[0]
    piece_rows = factor_b.shape[1] // pieces_two
    slab_one = piece_rows * pieces_one
    logical_b = factor_b.reshape(grid_j, pieces_two, piece_rows, rank_width)[:, owner_two].reshape(-1, rank_width)
    logical_c = factor_c.reshape(-1, rank_width)
    gram_b = jnp.dot(logical_b.T.astype(jnp.float32), logical_b.astype(jnp.float32), precision=highest, preferred_element_type=jnp.float32)
    gram_c = jnp.dot(logical_c.T.astype(jnp.float32), logical_c.astype(jnp.float32), precision=highest, preferred_element_type=jnp.float32)
    half_b = logical_b.astype(jnp.bfloat16)
    half_c = logical_c.astype(jnp.bfloat16)
    blocks_one = slab_one // block_edge
    blocks_two = factor_b.shape[1] // block_edge
    blocks_three = factor_c.shape[1] // block_edge
    total = grid_i * grid_j * grid_k * slot_count
    index_i = jnp.arange(grid_i, dtype=jnp.int32)[:, None, None, None]
    index_j = jnp.arange(grid_j, dtype=jnp.int32)[None, :, None, None]
    index_k = jnp.arange(grid_k, dtype=jnp.int32)[None, None, :, None]
    index_s = jnp.arange(slot_count, dtype=jnp.int32)[None, None, None, :]
    first = ((index_i * blocks_one + first_mode_rows) * block_edge).astype(jnp.int32).reshape(total)
    second = ((index_j * blocks_two + second_mode_rows) * block_edge).astype(jnp.int32).reshape(total)
    third = ((index_k * blocks_three + third_mode_rows) * block_edge).astype(jnp.int32).reshape(total)
    live = (index_s < filled[..., None]).astype(jnp.float32).reshape(total)
    flat_blocks = blocks.reshape(total, block_edge, block_edge, block_edge)
    rows_total_one = slab_one * grid_i
    rows_total_two = factor_b.shape[1] * grid_j

    def step_one(accum, item):
        block, start_one, start_two, start_three, weight = item
        b_rows = lax.dynamic_slice_in_dim(half_b, start_two, block_edge, 0)
        c_rows = lax.dynamic_slice_in_dim(half_c, start_three, block_edge, 0)
        inner = jnp.dot(block.reshape(block_edge * block_edge, block_edge).astype(jnp.float32), c_rows.astype(jnp.float32), preferred_element_type=jnp.float32)
        inner = inner.reshape(block_edge, block_edge, rank_width)
        contrib = batched_sum(inner, b_rows) * weight
        return (add_rows(accum, start_one, contrib), None)
    start_one = jnp.zeros((rows_total_one, rank_width), jnp.float32)
    mttkrp_one = lax.scan(step_one, start_one, (flat_blocks, first, second, third, live))[0]
    a_hat = solve_rows(gram_b * gram_c, mttkrp_one)
    scale_a = jnp.sqrt(lax.optimization_barrier(jnp.sum(a_hat * a_hat, axis=0)) / rows_total_one + EPS)
    a_logical = a_hat / scale_a
    gram_a = jnp.dot(a_logical.T.astype(jnp.float32), a_logical.astype(jnp.float32), precision=highest, preferred_element_type=jnp.float32)
    half_a = a_logical.astype(jnp.bfloat16)

    def step_two(accum, item):
        block, start_one, start_two, start_three, weight = item
        a_rows = lax.dynamic_slice_in_dim(half_a, start_one, block_edge, 0)
        c_rows = lax.dynamic_slice_in_dim(half_c, start_three, block_edge, 0)
        inner = lax.dot_general(block.reshape(block_edge, block_edge * block_edge).astype(jnp.float32), a_rows.astype(jnp.float32), (((0,), (0,)), ((), ())), preferred_element_type=jnp.float32)
        inner = inner.reshape(block_edge, block_edge, rank_width)
        contrib = batched_sum(inner, c_rows) * weight
        return (add_rows(accum, start_two, contrib), None)
    start_two = jnp.zeros((rows_total_two, rank_width), jnp.float32)
    mttkrp_two = lax.scan(step_two, start_two, (flat_blocks, first, second, third, live))[0]
    b_hat = solve_rows(gram_a * gram_c, mttkrp_two)
    scale_b = jnp.sqrt(lax.optimization_barrier(jnp.sum(b_hat * b_hat, axis=0)) / rows_total_two + EPS)
    b_logical = b_hat / scale_b
    inverse_one = jnp.argsort(owner_one).astype(jnp.int32)
    inverse_two = jnp.argsort(owner_two).astype(jnp.int32)
    a_new = a_logical.reshape(grid_i, pieces_one, piece_rows, rank_width)[:, inverse_one].reshape(grid_i, slab_one, rank_width)
    b_new = b_logical.reshape(grid_j, pieces_two, piece_rows, rank_width)[:, inverse_two].reshape(grid_j, -1, rank_width)
    return (a_new, b_new)
```

```python
import functools

import jax
import jax.numpy as jnp
from jax import lax
from jax.experimental import pallas as pl
from jax.experimental.pallas import tpu as pltpu
from jax.sharding import PartitionSpec as P

EPS = 1e-06
HALF = 128
GROUP = 8
MESH = pl.DeviceIdType.MESH
F32 = jnp.float32


def rem(a, b):
    return lax.rem(a, jnp.int32(b))


def div(a, b):
    return lax.div(a, jnp.int32(b))


def dot(a, b):
    return jnp.dot(a, b, precision=lax.Precision.HIGHEST, preferred_element_type=F32)


def dot_nt(a, b):
    return lax.dot_general(
        a, b, (((1,), (1,)), ((), ())), precision=lax.Precision.HIGHEST, preferred_element_type=F32
    )


def inverse_half(mat):
    lane = lax.broadcasted_iota(jnp.int32, (GROUP, HALF), 1)
    sub = lax.broadcasted_iota(jnp.int32, (GROUP, HALF), 0)
    lane_rest = lax.broadcasted_iota(jnp.int32, (HALF - GROUP, HALF), 1)

    def step(_, mat):
        top, rest = mat[:GROUP], mat[GROUP:]
        for s in range(GROUP):
            column = jnp.broadcast_to(top[:, s : s + 1], (GROUP, HALF))
            inv = 1.0 / column[s : s + 1]
            row = jnp.where(lane[:1] == s, 1.0, top[s : s + 1]) * inv
            cleared = jnp.where(lane == s, 0.0, top)
            top = jnp.where(sub == s, row, cleared - column * row)
        out = jnp.where(lane_rest < GROUP, 0.0, rest)
        for s in range(GROUP):
            out = out - rest[:, s : s + 1] * top[s : s + 1]
        return pltpu.roll(jnp.concatenate([out, top], axis=0), HALF - GROUP, 1)

    return lax.fori_loop(0, HALF // GROUP, step, mat)


def kernel(
    sizes,
    third,
    rows_b,
    rows_a,
    spots_one,
    spots_two,
    x_hbm,
    b_own,
    c_slab,
    a_out,
    b_out,
    x_buf,
    inner,
    gathered_b,
    gathered_a,
    rows_f32,
    contrib,
    part1,
    core1,
    line1,
    zed1,
    part2,
    core2,
    line2,
    zed2,
    local1,
    gram1,
    mix1,
    full1,
    local2,
    gram2,
    mix2,
    full2,
    own1,
    own2,
    gram_c_own,
    sq_ka,
    sq_kb,
    sq_la,
    sq_lb,
    factor,
    copy_sem,
    send_sem,
    recv_sem,
):
    n_i, n_j, n_k = sizes
    n_z = n_k // 2
    piece, rank = b_own.shape
    edge = x_hbm.shape[-1]
    per_block = edge // piece
    total_rows = n_i * n_j * n_k * piece
    chunk = rank // n_k
    i, j, k = lax.axis_index("ia"), lax.axis_index("ja"), lax.axis_index("ka")
    core = rem(k, 2)
    z = div(k, 2)
    plane = i * n_j + j
    n_plane = n_i * n_j
    sends = []

    def send(src, dst, where, stage):
        pltpu.make_async_remote_copy(
            src_ref=src,
            dst_ref=dst,
            send_sem=send_sem.at[stage],
            recv_sem=recv_sem.at[stage],
            device_id=where,
            device_id_type=MESH,
        ).start()

    def arrived(like, stage):
        pltpu.make_async_copy(like, like, recv_sem.at[stage]).wait()

    def at_plane(g):
        return {"ia": div(g, n_j), "ja": rem(g, n_j)}

    def gather_z(buf, line, n_line, stage):
        mine = buf.at[(core * n_line + line) * n_z + z]

        def one(d, carry):
            send(mine, mine, {"ka": rem(z + d, n_z) * 2 + core}, stage)
            return carry

        lax.fori_loop(1, n_z, one, 0)
        sends.append((buf.at[pl.ds(0, n_z - 1)], stage))

    def gather_line(buf, axis, line, n_line, stage):
        arrived(buf.at[pl.ds(0, n_z - 1)], stage - 1)
        mine = buf.at[pl.ds((core * n_line + line) * n_z, n_z)]

        def one(d, carry):
            send(mine, mine, {axis: rem(line + d, n_line)}, stage)
            return carry

        lax.fori_loop(1, n_line, one, 0)
        sends.append((buf.at[pl.ds(0, (n_line - 1) * n_z)], stage))

    def gather_core(buf, n_line, stage):
        half = n_line * n_z
        arrived(buf.at[pl.ds(0, half - n_z)], stage - 1)
        mine = buf.at[pl.ds(core * half, half)]
        send(mine, mine, {"ka": z * 2 + 1 - core}, stage)
        sends.append((buf.at[pl.ds(0, half)], stage))

    def scatter_core(part, got, stage):
        half = got.shape[0]
        send(part.at[pl.ds((1 - core) * half, half)], got, {"ka": z * 2 + 1 - core}, stage)
        sends.append((got, stage))

    def scatter_line(part, got_core, got, axis, line, n_line, stage):
        arrived(got_core, stage - 1)
        half = n_line * n_z

        def add(p, carry):
            part[core * half + p] = part[core * half + p] + got_core[p]
            return carry

        lax.fori_loop(0, half, add, 0)

        def one(d, carry):
            to = rem(line + d, n_line)
            send(part.at[pl.ds(core * half + to * n_z, n_z)], got.at[d - 1], {axis: to}, stage)
            return carry

        lax.fori_loop(1, n_line, one, 0)
        sends.append((got, stage))

    def scatter_z(part, got_line, got, line, n_line, stage):
        arrived(got_line, stage - 1)
        base = (core * n_line + line) * n_z

        def add(p, carry):
            value = part[base + p]
            for d in range(n_line - 1):
                value = value + got_line[d, p]
            part[base + p] = value
            return carry

        lax.fori_loop(0, n_z, add, 0)

        def one(d, carry):
            to = rem(z + d, n_z)
            send(part.at[base + to], got.at[d - 1], {"ka": to * 2 + core}, stage)
            return carry

        lax.fori_loop(1, n_z, one, 0)
        sends.append((got, stage))

    def scatter_end(part, got, line, n_line, stage):
        arrived(got, stage - 1)
        value = part[(core * n_line + line) * n_z + z]
        for d in range(n_z - 1):
            value = value + got[d]
        return value

    def share_k(source, got, stage):
        def one(d, carry):
            send(source(rem(k + d, n_k)), got.at[d - 1], {"ka": rem(k + d, n_k)}, stage)
            return carry

        lax.fori_loop(1, n_k, one, 0)
        sends.append((got, stage))

    def share_plane(source, got, stage):
        def one(d, carry):
            send(source, got.at[d - 1], at_plane(rem(plane + d, n_plane)), stage)
            return carry

        lax.fori_loop(1, n_plane, one, 0)
        sends.append((got, stage))

    def total(value, got, stage):
        arrived(got, stage)
        return lax.fori_loop(0, got.shape[0], lambda d, acc: acc + got[d], value)

    def gram_chunks(rows, local, which):
        value = dot(rows.T, rows)
        local[:, which] = value.reshape(n_k, chunk, rank)

    def gather_gram(full, value, stage):
        full[k] = value

        def one(d, carry):
            send(full.at[k], full.at[k], {"ka": rem(k + d, n_k)}, stage)
            return carry

        lax.fori_loop(1, n_k, one, 0)
        sends.append((full.at[pl.ds(0, n_k - 1)], stage))

    def invert_first(full):
        mat = full[...].reshape(rank, rank)
        pinv = inverse_half(mat[:HALF, :HALF])
        cross = mat[:HALF, HALF:]
        w = dot(pinv, cross)
        factor[0] = pinv
        factor[1] = w
        factor[2] = mat[HALF:, HALF:] - dot(cross.T, w)

    def invert_second():
        factor[2] = inverse_half(factor[2])

    def solve(rows):
        left, right = rows[:, :HALF], rows[:, HALF:]
        w = factor[1]
        v = dot(dot(left, w) - right, factor[2])
        return jnp.concatenate([dot(left, factor[0]) + dot_nt(v, w), -v], axis=1)

    def normalized(hat, got_k, mine_k, got_p, mine_p, stage):
        mine_k[...] = jnp.sum((hat * hat).reshape(piece // 8, 8, rank), axis=0)
        share_k(lambda to: mine_k, got_k, stage)
        mine_p[...] = total(mine_k[...], got_k, stage)
        share_plane(mine_p, got_p, stage + 1)
        squares = jnp.sum(total(mine_p[...], got_p, stage + 1), axis=0, keepdims=True)
        return hat / jnp.sqrt(squares / total_rows + EPS)

    def make_inner(s):
        x_copy(s).wait()
        c_rows = c_slab[third[s]].astype(jnp.bfloat16)
        span = 8

        def one(n, carry):
            rows = x_buf[s, pl.ds(n * span, span)].reshape(span * edge, edge)
            value = jnp.dot(rows, c_rows, preferred_element_type=F32)
            inner[s, pl.ds(n * span, span)] = value.reshape(span, edge, rank)
            return carry

        lax.fori_loop(0, edge // span, one, 0)

    def x_copy(s):
        return pltpu.make_async_copy(x_hbm.at[s], x_buf.at[s], copy_sem.at[s])

    def load_rows(buf, table, s):
        for t in range(per_block):
            value = buf[table[s * per_block + t]]
            rows_f32[s, pl.ds(t * piece, piece)] = value.astype(F32)

    def mode_one(s):
        def one(n, carry):
            span = 8
            for h in range(rank // HALF):
                lanes = pl.ds(h * HALF, HALF)
                value = inner[s, pl.ds(n * span, span), :, lanes]
                summed = jnp.sum(value * rows_f32[s, :, lanes][None], axis=1)
                contrib[s * per_block + div(n * span, piece), pl.ds(pl.multiple_of(rem(n * span, piece), span), span), lanes] = summed
            return carry

        lax.fori_loop(0, edge // 8, one, 0)

    def mode_two(s):
        def one(n, acc):
            for u in range(8):
                acc = acc + inner[s, n * 8 + u] * rows_f32[s, pl.ds(n * 8 + u, 1), :]
            return acc

        acc = lax.fori_loop(0, edge // 8, one, jnp.zeros((edge, rank), F32))
        contrib[pl.ds(s * per_block, per_block)] = acc.reshape(per_block, piece, rank)

    def place(table, part):
        def one(q, carry):
            part[q] = contrib[table[q]] + contrib[table[part.shape[0] + q]]
            return carry

        lax.fori_loop(0, part.shape[0], one, 0)

    for s in range(2):
        x_copy(s).start()
    gathered_b[(core * n_i + i) * n_z + z] = b_own[...].astype(jnp.bfloat16)
    barrier = pltpu.get_barrier_semaphore()

    def greet_k(d, carry):
        pl.semaphore_signal(barrier, inc=1, device_id={"ka": rem(k + d, n_k)}, device_id_type=MESH)
        return carry

    def greet_plane(d, carry):
        pl.semaphore_signal(barrier, inc=1, device_id=at_plane(rem(plane + d, n_plane)), device_id_type=MESH)
        return carry

    lax.fori_loop(1, n_k, greet_k, 0)
    lax.fori_loop(1, n_plane, greet_plane, 0)
    pl.semaphore_wait(barrier, n_k + n_plane - 2)

    gather_z(gathered_b, i, n_i, 0)
    gram_chunks(b_own[...], local1, 0)
    gram_chunks(c_slab[div(plane, per_block), pl.ds(pl.multiple_of(rem(plane, per_block) * piece, piece), piece)], local1, 1)
    share_k(lambda to: local1.at[to], gram1, 3)
    gather_line(gathered_b, "ia", i, n_i, 1)
    make_inner(0)
    gather_core(gathered_b, n_i, 2)
    make_inner(1)
    own1[...] = total(local1[k], gram1, 3)
    share_plane(own1, mix1, 4)
    contrib[2 * per_block] = jnp.zeros((piece, rank), F32)
    arrived(gathered_b.at[pl.ds(0, n_i * n_z)], 2)
    for s in range(2):
        load_rows(gathered_b, rows_b, s)
        mode_one(s)
    place(spots_one, part1)
    scatter_core(part1, core1, 6)
    grams = total(own1[...], mix1, 4)
    gram_c_own[...] = grams[1]
    gather_gram(full1, grams[0] * grams[1], 5)
    scatter_line(part1, core1, line1, "ja", j, n_j, 7)
    arrived(full1.at[pl.ds(0, n_k - 1)], 5)
    invert_first(full1)
    scatter_z(part1, line1, zed1, j, n_j, 8)
    invert_second()
    a_hat = solve(scatter_end(part1, zed1, j, n_j, 9))
    a_rows = normalized(a_hat, sq_ka.at[0], sq_kb.at[0], sq_la.at[0], sq_lb.at[0], 9)
    a_out[...] = a_rows

    gathered_a[(core * n_j + j) * n_z + z] = a_rows.astype(jnp.bfloat16)
    gather_z(gathered_a, j, n_j, 11)
    gram_chunks(a_rows, local2, 0)
    share_k(lambda to: local2.at[to], gram2, 14)
    gather_line(gathered_a, "ja", j, n_j, 12)
    own2[...] = total(local2[k], gram2, 14)
    share_plane(own2, mix2, 15)
    gather_core(gathered_a, n_j, 13)
    arrived(gathered_a.at[pl.ds(0, n_j * n_z)], 13)
    for s in range(2):
        load_rows(gathered_a, rows_a, s)
        mode_two(s)
    place(spots_two, part2)
    scatter_core(part2, core2, 17)
    gather_gram(full2, total(own2[...], mix2, 15)[0] * gram_c_own[...], 16)
    scatter_line(part2, core2, line2, "ia", i, n_i, 18)
    arrived(full2.at[pl.ds(0, n_k - 1)], 16)
    invert_first(full2)
    scatter_z(part2, line2, zed2, i, n_i, 19)
    invert_second()
    b_hat = solve(scatter_end(part2, zed2, i, n_i, 20))
    b_out[...] = normalized(b_hat, sq_ka.at[1], sq_kb.at[1], sq_la.at[1], sq_lb.at[1], 20)

    for like, stage in sends:
        pltpu.make_async_copy(like, like, send_sem.at[stage]).wait()


def tables(coord, filled, owner, per_block, n_k):
    count = owner.shape[0]
    place = jnp.arange(count, dtype=jnp.int32)
    wanted = (coord[:, None] * per_block + jnp.arange(per_block, dtype=jnp.int32)).reshape(-1)
    stored = jnp.sum(jnp.where(wanted[:, None] == place, owner, 0), axis=1)
    half = count // 2
    n_z = n_k // 2
    at = rem(stored, 2) * half + div(stored, n_k) * n_z + div(rem(stored, n_k), 2)
    live = (jnp.arange(2, dtype=jnp.int32) < filled)[:, None, None]
    hit = jnp.logical_and(at.reshape(2, per_block, 1) == place, live)
    none = 2 * per_block
    spots = none + jnp.sum(jnp.where(hit, jnp.arange(none, dtype=jnp.int32).reshape(2, per_block, 1) - none, 0), axis=1)
    return at, spots.reshape(-1)


def solution(mesh):
    n_i, n_j, n_k = (mesh.shape[name] for name in ("ia", "ja", "ka"))
    n_z = n_k // 2
    sizes = (n_i, n_j, n_k)

    def body(blocks, first, second, third, filled, owner_one, owner_two, factor_b, factor_c):
        piece, rank = factor_b.shape[1:]
        edge = blocks.shape[-1]
        chunk = rank // n_k
        n_plane = n_i * n_j
        stages = 22

        def vmem(*shape, dtype=F32):
            return pltpu.VMEM(shape, dtype)

        def scatter_buffers(n_line):
            return [
                vmem(2 * n_line * n_z, piece, rank),
                vmem(n_line * n_z, piece, rank),
                vmem(n_line - 1, n_z, piece, rank),
                vmem(n_z - 1, piece, rank),
            ]

        def gram_buffers(count):
            return [
                vmem(n_k, count, chunk, rank),
                vmem(n_k - 1, count, chunk, rank),
                vmem(n_plane - 1, count, chunk, rank),
                vmem(n_k, chunk, rank),
            ]

        scratch = [
            vmem(2, edge, edge, edge, dtype=jnp.bfloat16),
            vmem(2, edge, edge, rank),
            vmem(2 * n_i * n_z, piece, rank, dtype=jnp.bfloat16),
            vmem(2 * n_j * n_z, piece, rank, dtype=jnp.bfloat16),
            vmem(2, edge, rank),
            vmem(2 * edge // piece + 1, piece, rank),
            *scatter_buffers(n_j),
            *scatter_buffers(n_i),
            *gram_buffers(2),
            *gram_buffers(1),
            vmem(2, chunk, rank),
            vmem(1, chunk, rank),
            vmem(chunk, rank),
            vmem(2, n_k - 1, 8, rank),
            vmem(2, 8, rank),
            vmem(2, n_plane - 1, 8, rank),
            vmem(2, 8, rank),
            vmem(3, HALF, HALF),
            pltpu.SemaphoreType.DMA((2,)),
            pltpu.SemaphoreType.DMA((stages,)),
            pltpu.SemaphoreType.DMA((stages,)),
        ]
        per_block = edge // piece
        rows_b, spots_two = tables(second.reshape(2), filled.reshape(1), owner_two, per_block, n_k)
        rows_a, spots_one = tables(first.reshape(2), filled.reshape(1), owner_one, per_block, n_k)
        smem = pl.BlockSpec(memory_space=pltpu.SMEM)
        whole = pl.BlockSpec(memory_space=pltpu.VMEM)
        a_own, b_own = pl.pallas_call(
            functools.partial(kernel, sizes),
            out_shape=[jax.ShapeDtypeStruct((piece, rank), F32)] * 2,
            in_specs=[smem] * 5 + [pl.BlockSpec(memory_space=pl.ANY), whole, whole],
            out_specs=[whole, whole],
            scratch_shapes=scratch,
            compiler_params=pltpu.CompilerParams(
                collective_id=0, has_side_effects=True, vmem_limit_bytes=62 * 1024 * 1024
            ),
            name="sweep",
        )(
            third.reshape(2),
            rows_b,
            rows_a,
            spots_one,
            spots_two,
            blocks.reshape(blocks.shape[3:]),
            factor_b[0],
            factor_c[0].reshape(-1, edge, rank),
        )
        return a_own[None], b_own[None]

    return jax.shard_map(
        body,
        mesh=mesh,
        in_specs=(
            P("ia", "ja", "ka", None, None, None, None),
            P("ia", "ja", "ka", None),
            P("ia", "ja", "ka", None),
            P("ia", "ja", "ka", None),
            P("ia", "ja", "ka"),
            P(),
            P(),
            P("ja", ("ia", "ka"), None),
            P("ka", None, None),
        ),
        out_specs=(P("ia", ("ja", "ka"), None), P("ja", ("ia", "ka"), None)),
        check_vma=False,
    )
```

```python
import functools

import jax
import jax.numpy as jnp
from jax import lax
from jax.experimental import pallas as pl
from jax.experimental.pallas import tpu as pltpu
from jax.sharding import PartitionSpec as P

EPS = 1e-06
HALF = 128
GROUP = 8
MESH = pl.DeviceIdType.MESH
F32 = jnp.float32


def rem(a, b):
    return lax.rem(a, jnp.int32(b))


def div(a, b):
    return lax.div(a, jnp.int32(b))


def dot(a, b):
    return jnp.dot(a, b, precision=lax.Precision.HIGHEST, preferred_element_type=F32)


def dot_nt(a, b):
    return lax.dot_general(
        a, b, (((1,), (1,)), ((), ())), precision=lax.Precision.HIGHEST, preferred_element_type=F32
    )


def inverse_half(mat):
    lane = lax.broadcasted_iota(jnp.int32, (GROUP, HALF), 1)
    sub = lax.broadcasted_iota(jnp.int32, (GROUP, HALF), 0)
    lane_rest = lax.broadcasted_iota(jnp.int32, (HALF - GROUP, HALF), 1)

    def step(_, mat):
        top, rest = mat[:GROUP], mat[GROUP:]
        spread = [jnp.broadcast_to(top[:, t : t + 1], (GROUP, HALF)) for t in range(GROUP)]
        for s in range(GROUP):
            column = spread[s]
            inv = 1.0 / column[s : s + 1]
            row = jnp.where(lane[:1] == s, 1.0, top[s : s + 1]) * inv
            top = jnp.where(sub == s, row, jnp.where(lane == s, 0.0, top) - column * row)
            for t in range(s + 1, GROUP):
                entry = spread[t][s : s + 1] * inv
                spread[t] = jnp.where(sub == s, entry, spread[t] - column * entry)
        out = jnp.where(lane_rest < GROUP, 0.0, rest)
        for s in range(GROUP):
            out = out - rest[:, s : s + 1] * top[s : s + 1]
        return pltpu.roll(jnp.concatenate([out, top], axis=0), HALF - GROUP, 1)

    return lax.fori_loop(0, HALF // GROUP, step, mat)


def kernel(
    sizes,
    filled,
    first,
    second,
    third,
    owner_one,
    owner_two,
    x_hbm,
    b_own,
    c_slab,
    a_out,
    b_out,
    x_buf,
    inner,
    gathered_b,
    gathered_a,
    rows_f32,
    contrib,
    part1,
    core1,
    line1,
    zed1,
    part2,
    core2,
    line2,
    zed2,
    local1,
    gram1,
    mix1,
    full1,
    local2,
    gram2,
    mix2,
    full2,
    own1,
    own2,
    gram_c_own,
    sq_ka,
    sq_kb,
    sq_la,
    sq_lb,
    factor,
    spots_one,
    spots_two,
    copy_sem,
    send_sem,
    recv_sem,
):
    n_i, n_j, n_k = sizes
    n_z = n_k // 2
    piece, rank = b_own.shape
    edge = x_hbm.shape[-1]
    per_block = edge // piece
    total_rows = n_i * n_j * n_k * piece
    chunk = rank // n_k
    i, j, k = lax.axis_index("ia"), lax.axis_index("ja"), lax.axis_index("ka")
    core = rem(k, 2)
    z = div(k, 2)
    plane = i * n_j + j
    n_plane = n_i * n_j
    sends = []

    def sent(pair):
        sends.append(pair)

    def send(src, dst, where, stage):
        pltpu.make_async_remote_copy(
            src_ref=src,
            dst_ref=dst,
            send_sem=send_sem.at[stage],
            recv_sem=recv_sem.at[stage],
            device_id=where,
            device_id_type=MESH,
        ).start()

    def arrived(like, stage):
        pltpu.make_async_copy(like, like, recv_sem.at[stage]).wait()

    def at_plane(g):
        return {"ia": div(g, n_j), "ja": rem(g, n_j)}

    def gather_z(buf, line, n_line, stage):
        mine = buf.at[(core * n_line + line) * n_z + z]

        def one(d, carry):
            send(mine, mine, {"ka": rem(z + d, n_z) * 2 + core}, stage)
            return carry

        lax.fori_loop(1, n_z, one, 0)
        sent((buf.at[pl.ds(0, n_z - 1)], stage))

    def gather_line(buf, axis, line, n_line, stage, lines):
        arrived(buf.at[pl.ds(0, n_z - 1)], stage - 1)
        mine = buf.at[pl.ds((core * n_line + line) * n_z, n_z)]
        for d in range(1, n_line):
            send(mine, mine, {axis: rem(line + d, n_line)}, lines + d)
            sent((buf.at[pl.ds(0, n_z)], lines + d))
        send(mine, mine, {"ka": z * 2 + 1 - core}, stage)

    def gather_core(buf, line, n_line, stage, lines):
        for d in sorted(range(1, n_line), key=lambda d: min(d, n_line - d)):
            arrived(buf.at[pl.ds(0, n_z)], lines + d)
            mine = buf.at[pl.ds((core * n_line + rem(line + n_line - d, n_line)) * n_z, n_z)]
            send(mine, mine, {"ka": z * 2 + 1 - core}, stage)
        sent((buf.at[pl.ds(0, n_line * n_z)], stage))

    def scatter_core(part, got, stage):
        half = got.shape[0]
        send(part.at[pl.ds((1 - core) * half, half)], got, {"ka": z * 2 + 1 - core}, stage)
        sent((got, stage))

    def scatter_line(part, got_core, got, axis, line, n_line, stage):
        arrived(got_core, stage - 1)
        half = n_line * n_z

        def add(p, carry):
            part[core * half + p] = part[core * half + p] + got_core[p]
            return carry

        lax.fori_loop(0, half, add, 0)

        def one(d, carry):
            to = rem(line + d, n_line)
            send(part.at[pl.ds(core * half + to * n_z, n_z)], got.at[d - 1], {axis: to}, stage)
            return carry

        lax.fori_loop(1, n_line, one, 0)
        sent((got, stage))

    def scatter_z(part, got_line, got, line, n_line, stage):
        arrived(got_line, stage - 1)
        base = (core * n_line + line) * n_z

        def add(p, carry):
            value = part[base + p]
            for d in range(n_line - 1):
                value = value + got_line[d, p]
            part[base + p] = value
            return carry

        lax.fori_loop(0, n_z, add, 0)

        def one(d, carry):
            to = rem(z + d, n_z)
            send(part.at[base + to], got.at[d - 1], {"ka": to * 2 + core}, stage)
            return carry

        lax.fori_loop(1, n_z, one, 0)
        sent((got, stage))

    def scatter_end(part, got, line, n_line, stage):
        arrived(got, stage - 1)
        value = part[(core * n_line + line) * n_z + z]
        for d in range(n_z - 1):
            value = value + got[d]
        return value

    def share_k(source, got, stage):
        def one(d, carry):
            send(source(rem(k + d, n_k)), got.at[d - 1], {"ka": rem(k + d, n_k)}, stage)
            return carry

        lax.fori_loop(1, n_k, one, 0)
        sent((got, stage))

    def share_plane(source, got, stage):
        def one(d, carry):
            send(source, got.at[d - 1], at_plane(rem(plane + d, n_plane)), stage)
            return carry

        lax.fori_loop(1, n_plane, one, 0)
        sent((got, stage))

    def total(value, got, stage):
        arrived(got, stage)
        return lax.fori_loop(0, got.shape[0], lambda d, acc: acc + got[d], value)

    def gram_chunks(rows, local, which):
        value = dot(rows.T, rows)
        local[:, which] = value.reshape(n_k, chunk, rank)

    def gather_gram(full, value, stage):
        full[k] = value

        def one(d, carry):
            send(full.at[k], full.at[k], {"ka": rem(k + d, n_k)}, stage)
            return carry

        lax.fori_loop(1, n_k, one, 0)
        sent((full.at[pl.ds(0, n_k - 1)], stage))

    def invert_first(full):
        mat = full[...].reshape(rank, rank)
        pinv = inverse_half(mat[:HALF, :HALF])
        cross = mat[:HALF, HALF:]
        w = dot(pinv, cross)
        factor[0] = pinv
        factor[1] = w
        factor[2] = mat[HALF:, HALF:] - dot(cross.T, w)

    def invert_second():
        factor[2] = inverse_half(factor[2])

    def solve(rows):
        left, right = rows[:, :HALF], rows[:, HALF:]
        w = factor[1]
        v = dot(dot(left, w) - right, factor[2])
        return jnp.concatenate([dot(left, factor[0]) + dot_nt(v, w), -v], axis=1)

    def normalized(hat, got_k, mine_k, got_p, mine_p, stage):
        mine_k[...] = jnp.sum((hat * hat).reshape(piece // 8, 8, rank), axis=0)
        share_k(lambda to: mine_k, got_k, stage)
        mine_p[...] = total(mine_k[...], got_k, stage)
        share_plane(mine_p, got_p, stage + 1)
        squares = jnp.sum(total(mine_p[...], got_p, stage + 1), axis=0, keepdims=True)
        return hat / jnp.sqrt(squares / total_rows + EPS)

    def make_inner(s):
        x_copy(s).wait()
        c_rows = c_slab[third[s]].astype(jnp.bfloat16)
        span = 8

        def one(n, carry):
            rows = x_buf[s, pl.ds(n * span, span)].reshape(span * edge, edge)
            value = jnp.dot(rows, c_rows, preferred_element_type=F32)
            inner[s, pl.ds(n * span, span)] = value.reshape(span, edge, rank)
            return carry

        lax.fori_loop(0, edge // span, one, 0)

    def x_copy(s):
        return pltpu.make_async_copy(x_hbm.at[s], x_buf.at[s], copy_sem.at[s])

    def position(stored, n_line):
        return (rem(stored, 2) * n_line + div(stored, n_k)) * n_z + div(rem(stored, n_k), 2)

    def load_rows(buf, coord, owner, n_line, s):
        for t in range(per_block):
            value = buf[position(owner[coord[s] * per_block + t], n_line)]
            rows_f32[s, pl.ds(t * piece, piece)] = value.astype(F32)

    def mode_one(s):
        def one(n, carry):
            span = 8
            for h in range(rank // HALF):
                lanes = pl.ds(h * HALF, HALF)
                value = inner[s, pl.ds(n * span, span), :, lanes]
                summed = jnp.sum(value * rows_f32[s, :, lanes][None], axis=1)
                contrib[s * per_block + div(n * span, piece), pl.ds(pl.multiple_of(rem(n * span, piece), span), span), lanes] = summed
            return carry

        lax.fori_loop(0, edge // 8, one, 0)

    def mode_two(s):
        def one(n, acc):
            for u in range(8):
                acc = acc + inner[s, n * 8 + u] * rows_f32[s, pl.ds(n * 8 + u, 1), :]
            return acc

        acc = lax.fori_loop(0, edge // 8, one, jnp.zeros((edge, rank), F32))
        contrib[pl.ds(s * per_block, per_block)] = acc.reshape(per_block, piece, rank)

    def find_spots(spots, coord, owner, n_line):
        count = owner.shape[0]
        none = 2 * per_block
        wanted = [[position(owner[coord[s] * per_block + t], n_line) for t in range(per_block)] for s in range(2)]
        live = [(s < filled[0]).astype(jnp.int32) for s in range(2)]

        def one(q, carry):
            for s in range(2):
                at = jnp.int32(none)
                for t in range(per_block):
                    hit = (wanted[s][t] == q).astype(jnp.int32)
                    at = at + hit * live[s] * (s * per_block + t - none)
                spots[s * count + q] = at
            return carry

        lax.fori_loop(0, count, one, 0)

    def place(spots, part):
        count = part.shape[0]

        def one(q, carry):
            part[q] = contrib[spots[q]] + contrib[spots[count + q]]
            return carry

        lax.fori_loop(0, count, one, 0)

    for s in range(2):
        x_copy(s).start()
    gathered_b[(core * n_i + i) * n_z + z] = b_own[...].astype(jnp.bfloat16)
    barrier = pltpu.get_barrier_semaphore()

    def greet_k(d, carry):
        pl.semaphore_signal(barrier, inc=1, device_id={"ka": rem(k + d, n_k)}, device_id_type=MESH)
        return carry

    def greet_plane(d, carry):
        pl.semaphore_signal(barrier, inc=1, device_id=at_plane(rem(plane + d, n_plane)), device_id_type=MESH)
        return carry

    lax.fori_loop(1, n_k, greet_k, 0)
    lax.fori_loop(1, n_plane, greet_plane, 0)
    gram_chunks(b_own[...], local1, 0)
    gram_chunks(c_slab[div(plane, per_block), pl.ds(pl.multiple_of(rem(plane, per_block) * piece, piece), piece)], local1, 1)
    pl.semaphore_wait(barrier, n_k + n_plane - 2)

    gather_z(gathered_b, i, n_i, 0)
    share_k(lambda to: local1.at[to], gram1, 3)
    find_spots(spots_one, first, owner_one, n_j)
    find_spots(spots_two, second, owner_two, n_i)
    contrib[2 * per_block] = jnp.zeros((piece, rank), F32)
    gather_line(gathered_b, "ia", i, n_i, 1, 22)
    make_inner(0)
    gather_core(gathered_b, i, n_i, 1, 22)
    make_inner(1)
    arrived(gathered_b.at[pl.ds(0, n_i * n_z)], 1)
    load_rows(gathered_b, second, owner_two, n_i, 0)
    mode_one(0)
    own1[...] = total(local1[k], gram1, 3)
    share_plane(own1, mix1, 4)
    load_rows(gathered_b, second, owner_two, n_i, 1)
    mode_one(1)
    place(spots_one, part1)
    scatter_core(part1, core1, 6)
    grams = total(own1[...], mix1, 4)
    gram_c_own[...] = grams[1]
    gather_gram(full1, grams[0] * grams[1], 5)
    scatter_line(part1, core1, line1, "ja", j, n_j, 7)
    arrived(full1.at[pl.ds(0, n_k - 1)], 5)
    invert_first(full1)
    scatter_z(part1, line1, zed1, j, n_j, 8)
    invert_second()
    a_hat = solve(scatter_end(part1, zed1, j, n_j, 9))
    a_rows = normalized(a_hat, sq_ka.at[0], sq_kb.at[0], sq_la.at[0], sq_lb.at[0], 9)
    a_out[...] = a_rows

    gathered_a[(core * n_j + j) * n_z + z] = a_rows.astype(jnp.bfloat16)
    gather_z(gathered_a, j, n_j, 11)
    gram_chunks(a_rows, local2, 0)
    share_k(lambda to: local2.at[to], gram2, 14)
    gather_line(gathered_a, "ja", j, n_j, 12, 22 + n_i)
    own2[...] = total(local2[k], gram2, 14)
    share_plane(own2, mix2, 15)
    gather_core(gathered_a, j, n_j, 12, 22 + n_i)
    arrived(gathered_a.at[pl.ds(0, n_j * n_z)], 12)
    for s in range(2):
        load_rows(gathered_a, first, owner_one, n_j, s)
        mode_two(s)
    place(spots_two, part2)
    scatter_core(part2, core2, 17)
    gather_gram(full2, total(own2[...], mix2, 15)[0] * gram_c_own[...], 16)
    scatter_line(part2, core2, line2, "ia", i, n_i, 18)
    arrived(full2.at[pl.ds(0, n_k - 1)], 16)
    invert_first(full2)
    scatter_z(part2, line2, zed2, i, n_i, 19)
    invert_second()
    b_hat = solve(scatter_end(part2, zed2, i, n_i, 20))
    b_out[...] = normalized(b_hat, sq_ka.at[1], sq_kb.at[1], sq_la.at[1], sq_lb.at[1], 20)

    for like, stage in sends:
        pltpu.make_async_copy(like, like, send_sem.at[stage]).wait()


def solution(mesh):
    n_i, n_j, n_k = (mesh.shape[name] for name in ("ia", "ja", "ka"))
    n_z = n_k // 2
    sizes = (n_i, n_j, n_k)

    def body(blocks, first, second, third, filled, owner_one, owner_two, factor_b, factor_c):
        piece, rank = factor_b.shape[1:]
        edge = blocks.shape[-1]
        chunk = rank // n_k
        n_plane = n_i * n_j
        stages = 22 + n_i + n_j

        def vmem(*shape, dtype=F32):
            return pltpu.VMEM(shape, dtype)

        def scatter_buffers(n_line):
            return [
                vmem(2 * n_line * n_z, piece, rank),
                vmem(n_line * n_z, piece, rank),
                vmem(n_line - 1, n_z, piece, rank),
                vmem(n_z - 1, piece, rank),
            ]

        def gram_buffers(count):
            return [
                vmem(n_k, count, chunk, rank),
                vmem(n_k - 1, count, chunk, rank),
                vmem(n_plane - 1, count, chunk, rank),
                vmem(n_k, chunk, rank),
            ]

        scratch = [
            vmem(2, edge, edge, edge, dtype=jnp.bfloat16),
            vmem(2, edge, edge, rank),
            vmem(2 * n_i * n_z, piece, rank, dtype=jnp.bfloat16),
            vmem(2 * n_j * n_z, piece, rank, dtype=jnp.bfloat16),
            vmem(2, edge, rank),
            vmem(2 * edge // piece + 1, piece, rank),
            *scatter_buffers(n_j),
            *scatter_buffers(n_i),
            *gram_buffers(2),
            *gram_buffers(1),
            vmem(2, chunk, rank),
            vmem(1, chunk, rank),
            vmem(chunk, rank),
            vmem(2, n_k - 1, 8, rank),
            vmem(2, 8, rank),
            vmem(2, n_plane - 1, 8, rank),
            vmem(2, 8, rank),
            vmem(3, HALF, HALF),
            pltpu.SMEM((2 * owner_one.shape[0],), jnp.int32),
            pltpu.SMEM((2 * owner_two.shape[0],), jnp.int32),
            pltpu.SemaphoreType.DMA((2,)),
            pltpu.SemaphoreType.DMA((stages,)),
            pltpu.SemaphoreType.DMA((stages,)),
        ]
        smem = pl.BlockSpec(memory_space=pltpu.SMEM)
        whole = pl.BlockSpec(memory_space=pltpu.VMEM)
        a_own, b_own = pl.pallas_call(
            functools.partial(kernel, sizes),
            out_shape=[jax.ShapeDtypeStruct((piece, rank), F32)] * 2,
            in_specs=[smem] * 6 + [pl.BlockSpec(memory_space=pl.ANY), whole, whole],
            out_specs=[whole, whole],
            scratch_shapes=scratch,
            compiler_params=pltpu.CompilerParams(
                collective_id=0, has_side_effects=True, vmem_limit_bytes=62 * 1024 * 1024
            ),
            name="sweep",
        )(
            filled.reshape(1),
            first.reshape(2),
            second.reshape(2),
            third.reshape(2),
            owner_one,
            owner_two,
            blocks.reshape(blocks.shape[3:]),
            factor_b[0],
            factor_c[0].reshape(-1, edge, rank),
        )
        return a_own[None], b_own[None]

    return jax.shard_map(
        body,
        mesh=mesh,
        in_specs=(
            P("ia", "ja", "ka", None, None, None, None),
            P("ia", "ja", "ka", None),
            P("ia", "ja", "ka", None),
            P("ia", "ja", "ka", None),
            P("ia", "ja", "ka"),
            P(),
            P(),
            P("ja", ("ia", "ka"), None),
            P("ka", None, None),
        ),
        out_specs=(P("ia", ("ja", "ka"), None), P("ja", ("ia", "ka"), None)),
        check_vma=False,
    )
```

```python
import functools

import jax
import jax.numpy as jnp
from jax import lax
from jax.experimental import pallas as pl
from jax.experimental.pallas import tpu as pltpu
from jax.sharding import PartitionSpec as P

EPS = 1e-06
HALF = 128
GROUP = 8
MESH = pl.DeviceIdType.MESH
F32 = jnp.float32


def rem(a, b):
    return lax.rem(a, jnp.int32(b))


def div(a, b):
    return lax.div(a, jnp.int32(b))


def dot(a, b):
    return jnp.dot(a, b, precision=lax.Precision.HIGHEST, preferred_element_type=F32)


def dot_nt(a, b):
    return lax.dot_general(
        a, b, (((1,), (1,)), ((), ())), precision=lax.Precision.HIGHEST, preferred_element_type=F32
    )


def inverse_half(mat):
    lane = lax.broadcasted_iota(jnp.int32, (GROUP, HALF), 1)
    sub = lax.broadcasted_iota(jnp.int32, (GROUP, HALF), 0)
    lane_rest = lax.broadcasted_iota(jnp.int32, (HALF - GROUP, HALF), 1)

    def step(_, mat):
        top, rest = mat[:GROUP], mat[GROUP:]
        spread = [jnp.broadcast_to(top[:, t : t + 1], (GROUP, HALF)) for t in range(GROUP)]
        for s in range(GROUP):
            column = spread[s]
            inv = 1.0 / column[s : s + 1]
            row = jnp.where(lane[:1] == s, 1.0, top[s : s + 1]) * inv
            top = jnp.where(sub == s, row, jnp.where(lane == s, 0.0, top) - column * row)
            for t in range(s + 1, GROUP):
                entry = spread[t][s : s + 1] * inv
                spread[t] = jnp.where(sub == s, entry, spread[t] - column * entry)
        out = jnp.where(lane_rest < GROUP, 0.0, rest)
        for s in range(GROUP):
            out = out - rest[:, s : s + 1] * top[s : s + 1]
        return pltpu.roll(jnp.concatenate([out, top], axis=0), HALF - GROUP, 1)

    return lax.fori_loop(0, HALF // GROUP, step, mat)


def kernel(
    sizes,
    filled,
    first,
    second,
    third,
    owner_one,
    owner_two,
    x_hbm,
    b_own,
    c_slab,
    a_out,
    b_out,
    x_buf,
    inner,
    gathered_b,
    gathered_a,
    rows_f32,
    contrib,
    part1,
    core1,
    line1,
    zed1,
    part2,
    core2,
    line2,
    zed2,
    local1,
    gram1,
    mix1,
    full1,
    local2,
    gram2,
    mix2,
    full2,
    own1,
    own2,
    gram_c_own,
    sq_ka,
    sq_kb,
    sq_la,
    sq_lb,
    hats,
    factor,
    spots_one,
    spots_two,
    copy_sem,
    send_sem,
    recv_sem,
):
    n_i, n_j, n_k = sizes
    n_z = n_k // 2
    piece, rank = b_own.shape
    edge = x_hbm.shape[-1]
    per_block = edge // piece
    total_rows = n_i * n_j * n_k * piece
    chunk = rank // n_k
    i, j, k = lax.axis_index("ia"), lax.axis_index("ja"), lax.axis_index("ka")
    core = rem(k, 2)
    z = div(k, 2)
    plane = i * n_j + j
    n_plane = n_i * n_j
    sends = []

    def sent(pair):
        sends.append(pair)

    def send(src, dst, where, stage):
        pltpu.make_async_remote_copy(
            src_ref=src,
            dst_ref=dst,
            send_sem=send_sem.at[stage],
            recv_sem=recv_sem.at[stage],
            device_id=where,
            device_id_type=MESH,
        ).start()

    def arrived(like, stage):
        pltpu.make_async_copy(like, like, recv_sem.at[stage]).wait()

    def at_plane(g):
        return {"ia": div(g, n_j), "ja": rem(g, n_j)}

    def gather_z(buf, line, n_line, stage):
        mine = buf.at[(core * n_line + line) * n_z + z]

        def one(d, carry):
            send(mine, mine, {"ka": rem(z + d, n_z) * 2 + core}, stage)
            return carry

        lax.fori_loop(1, n_z, one, 0)
        sent((buf.at[pl.ds(0, n_z - 1)], stage))

    def gather_line(buf, axis, line, n_line, stage, lines):
        mine = buf.at[pl.ds((core * n_line + line) * n_z, n_z)]
        for d in range(1, n_line):
            send(mine, mine, {axis: rem(line + d, n_line)}, lines + d)
            sent((buf.at[pl.ds(0, n_z)], lines + d))
        send(mine, mine, {"ka": z * 2 + 1 - core}, stage)

    def gather_core(buf, line, n_line, stage, lines):
        for d in sorted(range(1, n_line), key=lambda d: min(d, n_line - d)):
            arrived(buf.at[pl.ds(0, n_z)], lines + d)
            mine = buf.at[pl.ds((core * n_line + rem(line + n_line - d, n_line)) * n_z, n_z)]
            send(mine, mine, {"ka": z * 2 + 1 - core}, stage)
        sent((buf.at[pl.ds(0, n_line * n_z)], stage))

    def scatter_core(part, got, stage):
        half = got.shape[0]
        send(part.at[pl.ds((1 - core) * half, half)], got, {"ka": z * 2 + 1 - core}, stage)
        sent((got, stage))

    def scatter_line(part, got_core, got, axis, line, n_line, stage):
        arrived(got_core, stage - 1)
        half = n_line * n_z

        def add(p, carry):
            part[core * half + p] = part[core * half + p] + got_core[p]
            return carry

        lax.fori_loop(0, half, add, 0)

        def one(d, carry):
            to = rem(line + d, n_line)
            send(part.at[pl.ds(core * half + to * n_z, n_z)], got.at[d - 1], {axis: to}, stage)
            return carry

        lax.fori_loop(1, n_line, one, 0)
        sent((got, stage))

    def scatter_z(part, got_line, got, line, n_line, stage):
        arrived(got_line, stage - 1)
        base = (core * n_line + line) * n_z

        def add(p, carry):
            value = part[base + p]
            for d in range(n_line - 1):
                value = value + got_line[d, p]
            part[base + p] = value
            return carry

        lax.fori_loop(0, n_z, add, 0)

        def one(d, carry):
            to = rem(z + d, n_z)
            send(part.at[base + to], got.at[d - 1], {"ka": to * 2 + core}, stage)
            return carry

        lax.fori_loop(1, n_z, one, 0)
        sent((got, stage))

    def scatter_end(part, got, line, n_line, stage):
        arrived(got, stage - 1)
        value = part[(core * n_line + line) * n_z + z]
        for d in range(n_z - 1):
            value = value + got[d]
        return value

    def share_k(source, got, stage):
        def one(d, carry):
            send(source(rem(k + d, n_k)), got.at[d - 1], {"ka": rem(k + d, n_k)}, stage)
            return carry

        lax.fori_loop(1, n_k, one, 0)
        sent((got, stage))

    def share_plane(source, got, stage):
        def one(d, carry):
            send(source, got.at[d - 1], at_plane(rem(plane + d, n_plane)), stage)
            return carry

        lax.fori_loop(1, n_plane, one, 0)
        sent((got, stage))

    def total(value, got, stage):
        arrived(got, stage)
        return lax.fori_loop(0, got.shape[0], lambda d, acc: acc + got[d], value)

    def gram_chunks(rows, local, which):
        value = dot(rows.T, rows)
        local[:, which] = value.reshape(n_k, chunk, rank)

    def gather_gram(full, value, stage):
        full[k] = value

        def one(d, carry):
            send(full.at[k], full.at[k], {"ka": rem(k + d, n_k)}, stage)
            return carry

        lax.fori_loop(1, n_k, one, 0)
        sent((full.at[pl.ds(0, n_k - 1)], stage))

    def invert_first(full):
        mat = full[...].reshape(rank, rank)
        pinv = inverse_half(mat[:HALF, :HALF])
        cross = mat[:HALF, HALF:]
        w = dot(pinv, cross)
        factor[0] = pinv
        factor[1] = w
        factor[2] = mat[HALF:, HALF:] - dot(cross.T, w)

    def invert_second():
        factor[2] = inverse_half(factor[2])

    def solve(rows):
        left, right = rows[:, :HALF], rows[:, HALF:]
        w = factor[1]
        v = dot(dot(left, w) - right, factor[2])
        return jnp.concatenate([dot(left, factor[0]) + dot_nt(v, w), -v], axis=1)

    def squares_start(hat, got_k, mine_k, stage):
        mine_k[...] = jnp.sum(hat * hat, axis=0, keepdims=True)
        share_k(lambda to: mine_k, got_k, stage)

    def scale_of(got_k, mine_k, got_p, mine_p, stage):
        mine_p[...] = total(mine_k[...], got_k, stage)
        share_plane(mine_p, got_p, stage + 1)
        return jnp.sqrt(total(mine_p[...], got_p, stage + 1) / total_rows + EPS)

    def make_inner(s):
        x_copy(s).wait()
        c_rows = c_slab[third[s]].astype(jnp.bfloat16)
        span = 8

        def one(n, carry):
            rows = x_buf[s, pl.ds(n * span, span)].reshape(span * edge, edge)
            value = jnp.dot(rows, c_rows, preferred_element_type=F32)
            inner[s, pl.ds(n * span, span)] = value.reshape(span, edge, rank)
            return carry

        lax.fori_loop(0, edge // span, one, 0)

    def x_copy(s):
        return pltpu.make_async_copy(x_hbm.at[s], x_buf.at[s], copy_sem.at[s])

    def position(stored, n_line):
        return (rem(stored, 2) * n_line + div(stored, n_k)) * n_z + div(rem(stored, n_k), 2)

    def load_rows(buf, coord, owner, n_line, s):
        for t in range(per_block):
            value = buf[position(owner[coord[s] * per_block + t], n_line)]
            rows_f32[s, pl.ds(t * piece, piece)] = value.astype(F32)

    def mode_one(s):
        def one(n, carry):
            span = 8
            for h in range(rank // HALF):
                lanes = pl.ds(h * HALF, HALF)
                value = inner[s, pl.ds(n * span, span), :, lanes]
                summed = jnp.sum(value * rows_f32[s, :, lanes][None], axis=1)
                contrib[s * per_block + div(n * span, piece), pl.ds(pl.multiple_of(rem(n * span, piece), span), span), lanes] = summed
            return carry

        lax.fori_loop(0, edge // 8, one, 0)

    def mode_two(s):
        def one(n, acc):
            for u in range(8):
                acc = acc + inner[s, n * 8 + u] * rows_f32[s, pl.ds(n * 8 + u, 1), :]
            return acc

        acc = lax.fori_loop(0, edge // 8, one, jnp.zeros((edge, rank), F32))
        contrib[pl.ds(s * per_block, per_block)] = acc.reshape(per_block, piece, rank)

    def find_spots(spots, coord, owner, n_line):
        count = owner.shape[0]
        none = 2 * per_block
        wanted = [[position(owner[coord[s] * per_block + t], n_line) for t in range(per_block)] for s in range(2)]
        live = [(s < filled[0]).astype(jnp.int32) for s in range(2)]

        def one(q, carry):
            for s in range(2):
                at = jnp.int32(none)
                for t in range(per_block):
                    hit = (wanted[s][t] == q).astype(jnp.int32)
                    at = at + hit * live[s] * (s * per_block + t - none)
                spots[s * count + q] = at
            return carry

        lax.fori_loop(0, count, one, 0)

    def place(spots, part):
        count = part.shape[0]

        def one(q, carry):
            part[q] = contrib[spots[q]] + contrib[spots[count + q]]
            return carry

        lax.fori_loop(0, count, one, 0)

    for s in range(2):
        x_copy(s).start()
    gathered_b[(core * n_i + i) * n_z + z] = b_own[...].astype(jnp.bfloat16)
    barrier = pltpu.get_barrier_semaphore()

    def greet_k(d, carry):
        pl.semaphore_signal(barrier, inc=1, device_id={"ka": rem(k + d, n_k)}, device_id_type=MESH)
        return carry

    def greet_plane(d, carry):
        pl.semaphore_signal(barrier, inc=1, device_id=at_plane(rem(plane + d, n_plane)), device_id_type=MESH)
        return carry

    lax.fori_loop(1, n_k, greet_k, 0)
    lax.fori_loop(1, n_plane, greet_plane, 0)
    gram_chunks(b_own[...], local1, 0)
    gram_chunks(c_slab[div(plane, per_block), pl.ds(pl.multiple_of(rem(plane, per_block) * piece, piece), piece)], local1, 1)
    pl.semaphore_wait(barrier, n_k + n_plane - 2)

    gather_z(gathered_b, i, n_i, 0)
    share_k(lambda to: local1.at[to], gram1, 3)
    find_spots(spots_one, first, owner_one, n_j)
    find_spots(spots_two, second, owner_two, n_i)
    contrib[2 * per_block] = jnp.zeros((piece, rank), F32)
    arrived(gathered_b.at[pl.ds(0, n_z - 1)], 0)
    gather_line(gathered_b, "ia", i, n_i, 1, 22)
    make_inner(0)
    gather_core(gathered_b, i, n_i, 1, 22)
    make_inner(1)
    arrived(gathered_b.at[pl.ds(0, n_i * n_z)], 1)
    load_rows(gathered_b, second, owner_two, n_i, 0)
    mode_one(0)
    own1[...] = total(local1[k], gram1, 3)
    share_plane(own1, mix1, 4)
    load_rows(gathered_b, second, owner_two, n_i, 1)
    mode_one(1)
    place(spots_one, part1)
    scatter_core(part1, core1, 6)
    grams = total(own1[...], mix1, 4)
    gram_c_own[...] = grams[1]
    gather_gram(full1, grams[0] * grams[1], 5)
    scatter_line(part1, core1, line1, "ja", j, n_j, 7)
    arrived(full1.at[pl.ds(0, n_k - 1)], 5)
    invert_first(full1)
    scatter_z(part1, line1, zed1, j, n_j, 8)
    invert_second()
    a_hat = solve(scatter_end(part1, zed1, j, n_j, 9))
    squares_start(a_hat, sq_ka.at[0], sq_kb.at[0], 9)
    hats[z] = a_hat

    def send_hat(d, carry):
        send(hats.at[z], hats.at[z], {"ka": rem(z + d, n_z) * 2 + core}, 11)
        return carry

    lax.fori_loop(1, n_z, send_hat, 0)
    sent((hats.at[pl.ds(0, n_z - 1)], 11))
    scale_a = scale_of(sq_ka.at[0], sq_kb.at[0], sq_la.at[0], sq_lb.at[0], 9)
    a_rows = a_hat / scale_a
    a_out[...] = a_rows

    arrived(hats.at[pl.ds(0, n_z - 1)], 11)

    def to_half(p, carry):
        gathered_a[(core * n_j + j) * n_z + p] = (hats[p] / scale_a).astype(jnp.bfloat16)
        return carry

    lax.fori_loop(0, n_z, to_half, 0)
    gather_line(gathered_a, "ja", j, n_j, 12, 22 + n_i)
    gram_chunks(a_rows, local2, 0)
    share_k(lambda to: local2.at[to], gram2, 14)
    own2[...] = total(local2[k], gram2, 14)
    share_plane(own2, mix2, 15)
    gather_core(gathered_a, j, n_j, 12, 22 + n_i)
    arrived(gathered_a.at[pl.ds(0, n_j * n_z)], 12)
    for s in range(2):
        load_rows(gathered_a, first, owner_one, n_j, s)
        mode_two(s)
    place(spots_two, part2)
    scatter_core(part2, core2, 17)
    gather_gram(full2, total(own2[...], mix2, 15)[0] * gram_c_own[...], 16)
    scatter_line(part2, core2, line2, "ia", i, n_i, 18)
    arrived(full2.at[pl.ds(0, n_k - 1)], 16)
    invert_first(full2)
    scatter_z(part2, line2, zed2, i, n_i, 19)
    invert_second()
    b_hat = solve(scatter_end(part2, zed2, i, n_i, 20))
    squares_start(b_hat, sq_ka.at[1], sq_kb.at[1], 20)
    b_out[...] = b_hat / scale_of(sq_ka.at[1], sq_kb.at[1], sq_la.at[1], sq_lb.at[1], 20)

    for like, stage in sends:
        pltpu.make_async_copy(like, like, send_sem.at[stage]).wait()


def solution(mesh):
    n_i, n_j, n_k = (mesh.shape[name] for name in ("ia", "ja", "ka"))
    n_z = n_k // 2
    sizes = (n_i, n_j, n_k)

    def body(blocks, first, second, third, filled, owner_one, owner_two, factor_b, factor_c):
        piece, rank = factor_b.shape[1:]
        edge = blocks.shape[-1]
        chunk = rank // n_k
        n_plane = n_i * n_j
        stages = 22 + n_i + n_j

        def vmem(*shape, dtype=F32):
            return pltpu.VMEM(shape, dtype)

        def scatter_buffers(n_line):
            return [
                vmem(2 * n_line * n_z, piece, rank),
                vmem(n_line * n_z, piece, rank),
                vmem(n_line - 1, n_z, piece, rank),
                vmem(n_z - 1, piece, rank),
            ]

        def gram_buffers(count):
            return [
                vmem(n_k, count, chunk, rank),
                vmem(n_k - 1, count, chunk, rank),
                vmem(n_plane - 1, count, chunk, rank),
                vmem(n_k, chunk, rank),
            ]

        scratch = [
            vmem(2, edge, edge, edge, dtype=jnp.bfloat16),
            vmem(2, edge, edge, rank),
            vmem(2 * n_i * n_z, piece, rank, dtype=jnp.bfloat16),
            vmem(2 * n_j * n_z, piece, rank, dtype=jnp.bfloat16),
            vmem(2, edge, rank),
            vmem(2 * edge // piece + 1, piece, rank),
            *scatter_buffers(n_j),
            *scatter_buffers(n_i),
            *gram_buffers(2),
            *gram_buffers(1),
            vmem(2, chunk, rank),
            vmem(1, chunk, rank),
            vmem(chunk, rank),
            vmem(2, n_k - 1, 1, rank),
            vmem(2, 1, rank),
            vmem(2, n_plane - 1, 1, rank),
            vmem(2, 1, rank),
            vmem(n_z, piece, rank),
            vmem(3, HALF, HALF),
            pltpu.SMEM((2 * owner_one.shape[0],), jnp.int32),
            pltpu.SMEM((2 * owner_two.shape[0],), jnp.int32),
            pltpu.SemaphoreType.DMA((2,)),
            pltpu.SemaphoreType.DMA((stages,)),
            pltpu.SemaphoreType.DMA((stages,)),
        ]
        smem = pl.BlockSpec(memory_space=pltpu.SMEM)
        whole = pl.BlockSpec(memory_space=pltpu.VMEM)
        a_own, b_own = pl.pallas_call(
            functools.partial(kernel, sizes),
            out_shape=[jax.ShapeDtypeStruct((piece, rank), F32)] * 2,
            in_specs=[smem] * 6 + [pl.BlockSpec(memory_space=pl.ANY), whole, whole],
            out_specs=[whole, whole],
            scratch_shapes=scratch,
            compiler_params=pltpu.CompilerParams(
                collective_id=0, has_side_effects=True, vmem_limit_bytes=62 * 1024 * 1024
            ),
            name="sweep",
        )(
            filled.reshape(1),
            first.reshape(2),
            second.reshape(2),
            third.reshape(2),
            owner_one,
            owner_two,
            blocks.reshape(blocks.shape[3:]),
            factor_b[0],
            factor_c[0].reshape(-1, edge, rank),
        )
        return a_own[None], b_own[None]

    return jax.shard_map(
        body,
        mesh=mesh,
        in_specs=(
            P("ia", "ja", "ka", None, None, None, None),
            P("ia", "ja", "ka", None),
            P("ia", "ja", "ka", None),
            P("ia", "ja", "ka", None),
            P("ia", "ja", "ka"),
            P(),
            P(),
            P("ja", ("ia", "ka"), None),
            P("ka", None, None),
        ),
        out_specs=(P("ia", ("ja", "ka"), None), P("ja", ("ia", "ka"), None)),
        check_vma=False,
    )
```

```python
import functools

import jax
import jax.numpy as jnp
from jax import lax
from jax.experimental import pallas as pl
from jax.experimental.pallas import tpu as pltpu
from jax.sharding import PartitionSpec as P

EPS = 1e-06
HALF = 128
GROUP = 8
MESH = pl.DeviceIdType.MESH
F32 = jnp.float32


def rem(a, b):
    return lax.rem(a, jnp.int32(b))


def div(a, b):
    return lax.div(a, jnp.int32(b))


def dot(a, b):
    return jnp.dot(a, b, precision=lax.Precision.HIGHEST, preferred_element_type=F32)


def dot_nt(a, b):
    return lax.dot_general(
        a, b, (((1,), (1,)), ((), ())), precision=lax.Precision.HIGHEST, preferred_element_type=F32
    )


def inverse_half(mat):
    lane = lax.broadcasted_iota(jnp.int32, (GROUP, HALF), 1)
    sub = lax.broadcasted_iota(jnp.int32, (GROUP, HALF), 0)
    lane_rest = lax.broadcasted_iota(jnp.int32, (HALF - GROUP, HALF), 1)

    def step(_, mat):
        top, rest = mat[:GROUP], mat[GROUP:]
        spread = [jnp.broadcast_to(top[:, t : t + 1], (GROUP, HALF)) for t in range(GROUP)]
        for s in range(GROUP):
            column = spread[s]
            inv = 1.0 / column[s : s + 1]
            row = jnp.where(lane[:1] == s, 1.0, top[s : s + 1]) * inv
            top = jnp.where(sub == s, row, jnp.where(lane == s, 0.0, top) - column * row)
            for t in range(s + 1, GROUP):
                entry = spread[t][s : s + 1] * inv
                spread[t] = jnp.where(sub == s, entry, spread[t] - column * entry)
        out = jnp.where(lane_rest < GROUP, 0.0, rest)
        for s in range(GROUP):
            out = out - rest[:, s : s + 1] * top[s : s + 1]
        return pltpu.roll(jnp.concatenate([out, top], axis=0), HALF - GROUP, 1)

    return lax.fori_loop(0, HALF // GROUP, step, mat)


def kernel(
    sizes,
    filled,
    first,
    second,
    third,
    owner_one,
    owner_two,
    x_hbm,
    b_own,
    c_slab,
    a_out,
    b_out,
    x_buf,
    x_far,
    c_own,
    c_send,
    c_far,
    info_send,
    info_got,
    info,
    b_send,
    hat_send,
    inner,
    gathered_b,
    gathered_a,
    rows_f32,
    contrib,
    part1,
    line1,
    zed1,
    part2,
    line2,
    zed2,
    local1,
    gram1,
    mix1,
    full1,
    local2,
    gram2,
    mix2,
    full2,
    own1,
    own2,
    gram_c_own,
    sq_ka,
    sq_kb,
    sq_la,
    sq_lb,
    hats,
    factor,
    spots_one,
    spots_two,
    copy_sem,
    send_sem,
    recv_sem,
):
    n_i, n_j, n_k = sizes
    piece, rank = b_own.shape
    edge = x_hbm.shape[-1]
    per_block = edge // piece
    total_rows = n_i * n_j * n_k * piece
    chunk = rank // n_k
    i, j, k = lax.axis_index("ia"), lax.axis_index("ja"), lax.axis_index("ka")
    core = rem(k, 2)
    plane = i * n_j + j
    n_plane = n_i * n_j
    sends = []

    def sent(pair):
        sends.append(pair)

    def send(src, dst, where, stage):
        pltpu.make_async_remote_copy(
            src_ref=src,
            dst_ref=dst,
            send_sem=send_sem.at[stage],
            recv_sem=recv_sem.at[stage],
            device_id=where,
            device_id_type=MESH,
        ).start()

    def arrived(like, stage):
        pltpu.make_async_copy(like, like, recv_sem.at[stage]).wait()

    def at_plane(g):
        return {"ia": div(g, n_j), "ja": rem(g, n_j)}

    def send_halves(source, target, stage):
        def one(d, carry):
            to = rem(k + d, n_k)
            send(source.at[rem(to, 2)], target, {"ka": to}, stage)
            return carry

        lax.fori_loop(1, n_k, one, 0)

    def gather_line(buf, axis, line, n_line, stage):
        mine = buf.at[pl.ds(line * n_k, n_k)]

        def one(d, carry):
            send(mine, mine, {axis: rem(line + d, n_line)}, stage)
            return carry

        lax.fori_loop(1, n_line, one, 0)
        sent((buf.at[pl.ds(0, (n_line - 1) * n_k)], stage))

    def scatter_line(part, got, axis, line, n_line, stage):
        def one(d, carry):
            to = rem(line + d, n_line)
            send(part.at[pl.ds(to * n_k, n_k)], got.at[d - 1], {axis: to}, stage)
            return carry

        lax.fori_loop(1, n_line, one, 0)
        sent((got, stage))

    def scatter_k(part, got_line, got, line, n_line, stage):
        arrived(got_line, stage - 1)
        base = line * n_k

        def add(p, carry):
            value = part[base + p]
            for d in range(n_line - 1):
                value = value + got_line[d, p]
            part[base + p] = value
            return carry

        lax.fori_loop(0, n_k, add, 0)

        def one(d, carry):
            to = rem(k + d, n_k)
            send(part.at[base + to], got.at[d - 1], {"ka": to}, stage)
            return carry

        lax.fori_loop(1, n_k, one, 0)
        sent((got, stage))

    def scatter_end(part, got, line, stage):
        arrived(got, stage)
        same = part[line * n_k + k]
        other = got[0]
        for d in range(2, n_k):
            if d % 2 == 0:
                same = same + got[d - 1]
            else:
                other = other + got[d - 1]
        return jnp.concatenate([jnp.where(core == 0, same, other), jnp.where(core == 0, other, same)], axis=1)

    def mine_of(value):
        return jnp.where(core == 0, value[:, :HALF], value[:, HALF:])

    def halves(buf, value):
        buf[0] = value[:, :HALF]
        buf[1] = value[:, HALF:]

    def share_k(source, got, stage):
        def one(d, carry):
            send(source(rem(k + d, n_k)), got.at[d - 1], {"ka": rem(k + d, n_k)}, stage)
            return carry

        lax.fori_loop(1, n_k, one, 0)
        sent((got, stage))

    def share_plane(source, got, stage):
        def one(d, carry):
            send(source, got.at[d - 1], at_plane(rem(plane + d, n_plane)), stage)
            return carry

        lax.fori_loop(1, n_plane, one, 0)
        sent((got, stage))

    def total(value, got, stage):
        arrived(got, stage)
        return lax.fori_loop(0, got.shape[0], lambda d, acc: acc + got[d], value)

    def gram_chunks(rows, local, which):
        value = dot(rows.T, rows)
        local[:, which] = value.reshape(n_k, chunk, rank)

    def gather_gram(full, value, stage):
        full[k] = value

        def one(d, carry):
            send(full.at[k], full.at[k], {"ka": rem(k + d, n_k)}, stage)
            return carry

        lax.fori_loop(1, n_k, one, 0)
        sent((full.at[pl.ds(0, n_k - 1)], stage))

    def invert_first(full):
        mat = full[...].reshape(rank, rank)
        pinv = inverse_half(mat[:HALF, :HALF])
        cross = mat[:HALF, HALF:]
        w = dot(pinv, cross)
        factor[0] = pinv
        factor[1] = w
        factor[2] = mat[HALF:, HALF:] - dot(cross.T, w)

    def invert_second():
        factor[2] = inverse_half(factor[2])

    def solve(rows):
        left, right = rows[:, :HALF], rows[:, HALF:]
        w = factor[1]
        v = dot(dot(left, w) - right, factor[2])
        return jnp.concatenate([dot(left, factor[0]) + dot_nt(v, w), -v], axis=1)

    def squares_start(hat, got_k, mine_k, stage):
        mine_k[...] = jnp.sum(hat * hat, axis=0, keepdims=True)
        share_k(lambda to: mine_k, got_k, stage)

    def scale_of(got_k, mine_k, got_p, mine_p, stage):
        mine_p[...] = total(mine_k[...], got_k, stage)
        share_plane(mine_p, got_p, stage + 1)
        return jnp.sqrt(total(mine_p[...], got_p, stage + 1) / total_rows + EPS)

    def make_inner(s):
        c_rows = c_own[s] if s < 2 else c_far[s - 2]
        x_rows = x_buf if s < 2 else x_far
        span = 8

        def one(n, carry):
            rows = x_rows[s % 2, pl.ds(n * span, span)].reshape(span * edge, edge)
            value = jnp.dot(rows, c_rows, preferred_element_type=F32)
            inner[s, pl.ds(n * span, span)] = value.reshape(span, edge, HALF)
            return carry

        lax.fori_loop(0, edge // span, one, 0)

    def x_copy(s):
        return pltpu.make_async_copy(x_hbm.at[s], x_buf.at[s], copy_sem.at[s])

    def coord_of(near, at, s):
        return near[s] if s < 2 else info[0, at + s - 2]

    def load_rows(buf, near, at, owner, s):
        coord = coord_of(near, at, s)
        for t in range(per_block):
            rows_f32[s, pl.ds(t * piece, piece)] = buf[owner[coord * per_block + t]].astype(F32)

    def mode_one(s):
        def one(n, carry):
            span = 8
            summed = jnp.sum(inner[s, pl.ds(n * span, span)] * rows_f32[s][None], axis=1)
            at = s * per_block + div(n * span, piece)
            contrib[at, pl.ds(pl.multiple_of(rem(n * span, piece), span), span)] = summed
            return carry

        lax.fori_loop(0, edge // 8, one, 0)

    def mode_two(s):
        def one(n, acc):
            for u in range(8):
                acc = acc + inner[s, n * 8 + u] * rows_f32[s, pl.ds(n * 8 + u, 1), :]
            return acc

        acc = lax.fori_loop(0, edge // 8, one, jnp.zeros((edge, HALF), F32))
        contrib[pl.ds(s * per_block, per_block)] = acc.reshape(per_block, piece, HALF)

    def find_spots(spots, near, at, owner):
        count = owner.shape[0]
        none = 4 * per_block
        wanted = [[owner[coord_of(near, at, s) * per_block + t] for t in range(per_block)] for s in range(4)]
        live = [(s < filled[0]).astype(jnp.int32) if s < 2 else info[0, s - 2] for s in range(4)]

        def one(q, carry):
            for s in range(4):
                spot = jnp.int32(none)
                for t in range(per_block):
                    hit = (wanted[s][t] == q).astype(jnp.int32)
                    spot = spot + hit * live[s] * (s * per_block + t - none)
                spots[s * count + q] = spot
            return carry

        lax.fori_loop(0, count, one, 0)

    def place(spots, part):
        count = part.shape[0]

        def one(q, carry):
            value = contrib[spots[q]]
            for s in range(1, 4):
                value = value + contrib[spots[s * count + q]]
            part[q] = value
            return carry

        lax.fori_loop(0, count, one, 0)

    for s in range(2):
        x_copy(s).start()
    b_half = b_own[...].astype(jnp.bfloat16)
    halves(b_send, b_half)
    gathered_b[i * n_k + k] = mine_of(b_half)
    lane = lax.broadcasted_iota(jnp.int32, info_send.shape, 1)
    told = jnp.zeros(info_send.shape, jnp.int32)
    for s in range(2):
        told = jnp.where(lane == s, (s < filled[0]).astype(jnp.int32), told)
        told = jnp.where(lane == 2 + s, first[s], told)
        told = jnp.where(lane == 4 + s, second[s], told)
        rows = c_slab[third[s]].astype(jnp.bfloat16)
        c_own[s] = mine_of(rows)
        c_send[s] = jnp.where(core == 0, rows[:, HALF:], rows[:, :HALF])
    info_send[...] = told
    barrier = pltpu.get_barrier_semaphore()

    def greet_k(d, carry):
        pl.semaphore_signal(barrier, inc=1, device_id={"ka": rem(k + d, n_k)}, device_id_type=MESH)
        return carry

    def greet_plane(d, carry):
        pl.semaphore_signal(barrier, inc=1, device_id=at_plane(rem(plane + d, n_plane)), device_id_type=MESH)
        return carry

    lax.fori_loop(1, n_k, greet_k, 0)
    lax.fori_loop(1, n_plane, greet_plane, 0)
    gram_chunks(b_own[...], local1, 0)
    gram_chunks(c_slab[div(plane, per_block), pl.ds(pl.multiple_of(rem(plane, per_block) * piece, piece), piece)], local1, 1)
    pl.semaphore_wait(barrier, n_k + n_plane - 2)

    partner = {"ka": k + 1 - 2 * core}
    send_halves(b_send, gathered_b.at[i * n_k + k], 0)
    sent((gathered_b.at[pl.ds(0, n_k - 1)], 0))
    send(info_send, info_got, partner, 12)
    sent((info_got, 12))
    send(c_send, c_far, partner, 6)
    sent((c_far, 6))
    for s in range(2):
        send(x_hbm.at[s], x_far.at[s], partner, 1 + s)
        sent((x_far.at[s], 1 + s))
    share_k(lambda to: local1.at[to], gram1, 3)
    contrib[4 * per_block] = jnp.zeros((piece, HALF), F32)
    arrived(gathered_b.at[pl.ds(0, n_k - 1)], 0)
    gather_line(gathered_b, "ia", i, n_i, 13)
    x_copy(0).wait()
    make_inner(0)
    x_copy(1).wait()
    make_inner(1)
    arrived(info_got, 12)
    copy = pltpu.make_async_copy(info_got, info, copy_sem.at[2])
    copy.start()
    copy.wait()
    find_spots(spots_one, first, 2, owner_one)
    find_spots(spots_two, second, 4, owner_two)
    arrived(gathered_b.at[pl.ds(0, (n_i - 1) * n_k)], 13)
    for s in range(2):
        load_rows(gathered_b, second, 4, owner_two, s)
        mode_one(s)
    arrived(c_far, 6)
    for s in range(2, 4):
        arrived(x_far.at[s - 2], s - 1)
        make_inner(s)
        load_rows(gathered_b, second, 4, owner_two, s)
        mode_one(s)
        if s == 2:
            own1[...] = total(local1[k], gram1, 3)
            share_plane(own1, mix1, 4)
    place(spots_one, part1)
    scatter_line(part1, line1, "ja", j, n_j, 7)
    grams = total(own1[...], mix1, 4)
    gram_c_own[...] = grams[1]
    gather_gram(full1, grams[0] * grams[1], 5)
    arrived(full1.at[pl.ds(0, n_k - 1)], 5)
    invert_first(full1)
    scatter_k(part1, line1, zed1, j, n_j, 8)
    invert_second()
    a_hat = solve(scatter_end(part1, zed1, j, 8))
    squares_start(a_hat, sq_ka.at[0], sq_kb.at[0], 9)
    halves(hat_send, a_hat)
    hats[k] = mine_of(a_hat)
    send_halves(hat_send, hats.at[k], 11)
    sent((hats.at[pl.ds(0, n_k - 1)], 11))
    scale_a = scale_of(sq_ka.at[0], sq_kb.at[0], sq_la.at[0], sq_lb.at[0], 9)
    scale_own = mine_of(scale_a)
    arrived(hats.at[pl.ds(0, n_k - 1)], 11)

    def to_half(p, carry):
        gathered_a[j * n_k + p] = (hats[p] / scale_own).astype(jnp.bfloat16)
        return carry

    lax.fori_loop(0, n_k, to_half, 0)
    gather_line(gathered_a, "ja", j, n_j, 17)
    a_rows = a_hat / scale_a
    a_out[...] = a_rows
    gram_chunks(a_rows, local2, 0)
    share_k(lambda to: local2.at[to], gram2, 14)
    arrived(gathered_a.at[pl.ds(0, (n_j - 1) * n_k)], 17)
    for s in range(4):
        load_rows(gathered_a, first, 2, owner_one, s)
        mode_two(s)
        if s == 2:
            own2[...] = total(local2[k], gram2, 14)
            share_plane(own2, mix2, 15)
    place(spots_two, part2)
    scatter_line(part2, line2, "ia", i, n_i, 18)
    gather_gram(full2, total(own2[...], mix2, 15)[0] * gram_c_own[...], 16)
    arrived(full2.at[pl.ds(0, n_k - 1)], 16)
    invert_first(full2)
    scatter_k(part2, line2, zed2, i, n_i, 19)
    invert_second()
    b_hat = solve(scatter_end(part2, zed2, i, 19))
    squares_start(b_hat, sq_ka.at[1], sq_kb.at[1], 20)
    b_out[...] = b_hat / scale_of(sq_ka.at[1], sq_kb.at[1], sq_la.at[1], sq_lb.at[1], 20)

    for like, stage in sends:
        pltpu.make_async_copy(like, like, send_sem.at[stage]).wait()


def solution(mesh):
    n_i, n_j, n_k = (mesh.shape[name] for name in ("ia", "ja", "ka"))
    sizes = (n_i, n_j, n_k)

    def body(blocks, first, second, third, filled, owner_one, owner_two, factor_b, factor_c):
        piece, rank = factor_b.shape[1:]
        edge = blocks.shape[-1]
        chunk = rank // n_k
        n_plane = n_i * n_j
        stages = 22

        def vmem(*shape, dtype=F32):
            return pltpu.VMEM(shape, dtype)

        def scatter_buffers(n_line):
            return [
                vmem(n_line * n_k, piece, HALF),
                vmem(n_line - 1, n_k, piece, HALF),
                vmem(n_k - 1, piece, HALF),
            ]

        def gram_buffers(count):
            return [
                vmem(n_k, count, chunk, rank),
                vmem(n_k - 1, count, chunk, rank),
                vmem(n_plane - 1, count, chunk, rank),
                vmem(n_k, chunk, rank),
            ]

        scratch = [
            vmem(2, edge, edge, edge, dtype=jnp.bfloat16),
            vmem(2, edge, edge, edge, dtype=jnp.bfloat16),
            vmem(2, edge, HALF, dtype=jnp.bfloat16),
            vmem(2, edge, HALF, dtype=jnp.bfloat16),
            vmem(2, edge, HALF, dtype=jnp.bfloat16),
            vmem(8, HALF, dtype=jnp.int32),
            vmem(8, HALF, dtype=jnp.int32),
            pltpu.SMEM((8, HALF), jnp.int32),
            vmem(2, piece, HALF, dtype=jnp.bfloat16),
            vmem(2, piece, HALF),
            vmem(4, edge, edge, HALF),
            vmem(n_i * n_k, piece, HALF, dtype=jnp.bfloat16),
            vmem(n_j * n_k, piece, HALF, dtype=jnp.bfloat16),
            vmem(4, edge, HALF),
            vmem(4 * edge // piece + 1, piece, HALF),
            *scatter_buffers(n_j),
            *scatter_buffers(n_i),
            *gram_buffers(2),
            *gram_buffers(1),
            vmem(2, chunk, rank),
            vmem(1, chunk, rank),
            vmem(chunk, rank),
            vmem(2, n_k - 1, 1, rank),
            vmem(2, 1, rank),
            vmem(2, n_plane - 1, 1, rank),
            vmem(2, 1, rank),
            vmem(n_k, piece, HALF),
            vmem(3, HALF, HALF),
            pltpu.SMEM((4 * owner_one.shape[0],), jnp.int32),
            pltpu.SMEM((4 * owner_two.shape[0],), jnp.int32),
            pltpu.SemaphoreType.DMA((3,)),
            pltpu.SemaphoreType.DMA((stages,)),
            pltpu.SemaphoreType.DMA((stages,)),
        ]
        smem = pl.BlockSpec(memory_space=pltpu.SMEM)
        whole = pl.BlockSpec(memory_space=pltpu.VMEM)
        a_own, b_own = pl.pallas_call(
            functools.partial(kernel, sizes),
            out_shape=[jax.ShapeDtypeStruct((piece, rank), F32)] * 2,
            in_specs=[smem] * 6 + [pl.BlockSpec(memory_space=pl.ANY), whole, whole],
            out_specs=[whole, whole],
            scratch_shapes=scratch,
            compiler_params=pltpu.CompilerParams(
                collective_id=0, has_side_effects=True, vmem_limit_bytes=62 * 1024 * 1024
            ),
            name="sweep",
        )(
            filled.reshape(1),
            first.reshape(2),
            second.reshape(2),
            third.reshape(2),
            owner_one,
            owner_two,
            blocks.reshape(blocks.shape[3:]),
            factor_b[0],
            factor_c[0].reshape(-1, edge, rank),
        )
        return a_own[None], b_own[None]

    return jax.shard_map(
        body,
        mesh=mesh,
        in_specs=(
            P("ia", "ja", "ka", None, None, None, None),
            P("ia", "ja", "ka", None),
            P("ia", "ja", "ka", None),
            P("ia", "ja", "ka", None),
            P("ia", "ja", "ka"),
            P(),
            P(),
            P("ja", ("ia", "ka"), None),
            P("ka", None, None),
        ),
        out_specs=(P("ia", ("ja", "ka"), None), P("ja", ("ia", "ka"), None)),
        check_vma=False,
    )
```

```python
import functools

import jax
import jax.numpy as jnp
from jax import lax
from jax.experimental import pallas as pl
from jax.experimental.pallas import tpu as pltpu
from jax.sharding import PartitionSpec as P

EPS = 1e-06
HALF = 128
GROUP = 8
MESH = pl.DeviceIdType.MESH
F32 = jnp.float32


def rem(a, b):
    return lax.rem(a, jnp.int32(b))


def div(a, b):
    return lax.div(a, jnp.int32(b))


def dot(a, b):
    return jnp.dot(a, b, precision=lax.Precision.HIGHEST, preferred_element_type=F32)


def dot_nt(a, b):
    return lax.dot_general(
        a, b, (((1,), (1,)), ((), ())), precision=lax.Precision.HIGHEST, preferred_element_type=F32
    )


def inverse_half(mat):
    lane = lax.broadcasted_iota(jnp.int32, (GROUP, HALF), 1)
    sub = lax.broadcasted_iota(jnp.int32, (GROUP, HALF), 0)
    lane_rest = lax.broadcasted_iota(jnp.int32, (HALF - GROUP, HALF), 1)

    def step(_, mat):
        top, rest = mat[:GROUP], mat[GROUP:]
        spread = [jnp.broadcast_to(top[:, t : t + 1], (GROUP, HALF)) for t in range(GROUP)]
        for s in range(GROUP):
            column = spread[s]
            inv = 1.0 / column[s : s + 1]
            row = jnp.where(lane[:1] == s, 1.0, top[s : s + 1]) * inv
            top = jnp.where(sub == s, row, jnp.where(lane == s, 0.0, top) - column * row)
            for t in range(s + 1, GROUP):
                entry = spread[t][s : s + 1] * inv
                spread[t] = jnp.where(sub == s, entry, spread[t] - column * entry)
        out = jnp.where(lane_rest < GROUP, 0.0, rest)
        for s in range(GROUP):
            out = out - rest[:, s : s + 1] * top[s : s + 1]
        return pltpu.roll(jnp.concatenate([out, top], axis=0), HALF - GROUP, 1)

    return lax.fori_loop(0, HALF // GROUP, step, mat)


def kernel(
    sizes,
    filled,
    first,
    second,
    third,
    owner_one,
    owner_two,
    x_hbm,
    b_own,
    c_slab,
    a_out,
    b_out,
    x_buf,
    inner,
    gathered_b,
    gathered_a,
    rows_f32,
    contrib,
    part1,
    core1,
    line1,
    zed1,
    part2,
    core2,
    line2,
    zed2,
    local1,
    gram1,
    mix1,
    full1,
    local2,
    gram2,
    mix2,
    full2,
    own1,
    own2,
    gram_c_own,
    sq_ka,
    sq_kb,
    sq_la,
    sq_lb,
    hats,
    factor,
    spots_one,
    spots_two,
    copy_sem,
    send_sem,
    recv_sem,
):
    n_i, n_j, n_k = sizes
    n_z = n_k // 2
    piece, rank = b_own.shape
    edge = x_hbm.shape[-1]
    per_block = edge // piece
    total_rows = n_i * n_j * n_k * piece
    chunk = rank // n_k
    i, j, k = lax.axis_index("ia"), lax.axis_index("ja"), lax.axis_index("ka")
    core = rem(k, 2)
    z = div(k, 2)
    plane = i * n_j + j
    n_plane = n_i * n_j
    sends = []
    extra = 22 + n_i + n_j
    extra2 = extra + n_j + n_z // 2

    def sent(pair):
        sends.append(pair)

    def send(src, dst, where, stage):
        pltpu.make_async_remote_copy(
            src_ref=src,
            dst_ref=dst,
            send_sem=send_sem.at[stage],
            recv_sem=recv_sem.at[stage],
            device_id=where,
            device_id_type=MESH,
        ).start()

    def arrived(like, stage):
        pltpu.make_async_copy(like, like, recv_sem.at[stage]).wait()

    def at_plane(g):
        return {"ia": div(g, n_j), "ja": rem(g, n_j)}

    def gather_z(buf, line, n_line, stage):
        mine = buf.at[(core * n_line + line) * n_z + z]

        def one(d, carry):
            send(mine, mine, {"ka": rem(z + d, n_z) * 2 + core}, stage)
            return carry

        lax.fori_loop(1, n_z, one, 0)
        sent((buf.at[pl.ds(0, n_z - 1)], stage))

    def gather_line(buf, axis, line, n_line, stage, lines):
        mine = buf.at[pl.ds((core * n_line + line) * n_z, n_z)]
        for d in range(1, n_line):
            send(mine, mine, {axis: rem(line + d, n_line)}, lines + d)
            sent((buf.at[pl.ds(0, n_z)], lines + d))
        send(mine, mine, {"ka": z * 2 + 1 - core}, stage)

    def gather_core(buf, line, n_line, stage, lines):
        for d in sorted(range(1, n_line), key=lambda d: min(d, n_line - d)):
            arrived(buf.at[pl.ds(0, n_z)], lines + d)
            mine = buf.at[pl.ds((core * n_line + rem(line + n_line - d, n_line)) * n_z, n_z)]
            send(mine, mine, {"ka": z * 2 + 1 - core}, stage)
        sent((buf.at[pl.ds(0, n_line * n_z)], stage))

    pair = 2

    def scatter_core(part, got, spots, line, n_line, stage):
        for d in [*range(1, n_line), 0]:
            at = rem(line + d, n_line) * n_z
            far = (1 - core) * n_line * n_z + at
            place(spots, part, far)
            send(part.at[pl.ds(far, n_z)], got.at[pl.ds(at, n_z)], {"ka": z * 2 + 1 - core}, stage + d)
            sent((got.at[pl.ds(0, n_z)], stage + d))
        for d in range(n_line):
            place(spots, part, (core * n_line + rem(line + d, n_line)) * n_z)

    def add_core(part, got_core, line, n_line, d, stage):
        at = rem(line + d, n_line) * n_z
        arrived(got_core.at[pl.ds(0, n_z)], stage + d)
        mine = pl.ds(core * n_line * n_z + at, n_z)
        part[mine] = part[mine] + got_core[pl.ds(at, n_z)]

    def scatter_line(part, got_core, got, axis, line, n_line, core_stage, stage):
        for d in range(1, n_line):
            add_core(part, got_core, line, n_line, d, core_stage)
            to = rem(line + d, n_line)
            base = (core * n_line + to) * n_z
            for g in range(n_z // pair):
                send(part.at[pl.ds(base + g * pair, pair)], got.at[g, d - 1], {axis: to}, stage + g)
        for g in range(n_z // pair):
            sent((got.at[g], stage + g))
        add_core(part, got_core, line, n_line, 0, core_stage)

    def scatter_z(part, got_line, got, line, n_line, line_stage, stage):
        base = (core * n_line + line) * n_z
        for g in range(n_z // pair):
            arrived(got_line.at[g], line_stage + g)
            group = pl.ds(base + g * pair, pair)
            value = part[group]
            for d in range(n_line - 1):
                value = value + got_line[g, d]
            part[group] = value
            for p in range(g * pair, (g + 1) * pair):
                if p < n_z - 1:
                    send(part.at[base + p], got.at[p], {"ka": rem(z + p + 1, n_z) * 2 + core}, stage)
        sent((got, stage))

    def scatter_end(part, got, line, n_line, stage):
        arrived(got, stage)
        value = part[(core * n_line + line) * n_z + n_z - 1]
        for d in range(n_z - 1):
            value = value + got[d]
        return value

    def share_k(source, got, stage):
        def one(d, carry):
            send(source(rem(k + d, n_k)), got.at[d - 1], {"ka": rem(k + d, n_k)}, stage)
            return carry

        lax.fori_loop(1, n_k, one, 0)
        sent((got, stage))

    def share_plane(source, got, stage):
        def one(d, carry):
            send(source, got.at[d - 1], at_plane(rem(plane + d, n_plane)), stage)
            return carry

        lax.fori_loop(1, n_plane, one, 0)
        sent((got, stage))

    def total(value, got, stage):
        arrived(got, stage)
        return lax.fori_loop(0, got.shape[0], lambda d, acc: acc + got[d], value)

    def gram_chunks(rows, local, which):
        value = dot(rows.T, rows)
        local[:, which] = value.reshape(n_k, chunk, rank)

    def gather_gram(full, value, stage):
        full[k] = value

        def one(d, carry):
            send(full.at[k], full.at[k], {"ka": rem(k + d, n_k)}, stage)
            return carry

        lax.fori_loop(1, n_k, one, 0)
        sent((full.at[pl.ds(0, n_k - 1)], stage))

    def invert_first(full):
        mat = full[...].reshape(rank, rank)
        pinv = inverse_half(mat[:HALF, :HALF])
        cross = mat[:HALF, HALF:]
        w = dot(pinv, cross)
        factor[0] = pinv
        factor[1] = w
        factor[2] = mat[HALF:, HALF:] - dot(cross.T, w)

    def invert_second():
        factor[2] = inverse_half(factor[2])

    def solve(rows):
        left, right = rows[:, :HALF], rows[:, HALF:]
        w = factor[1]
        v = dot(dot(left, w) - right, factor[2])
        return jnp.concatenate([dot(left, factor[0]) + dot_nt(v, w), -v], axis=1)

    def squares_start(hat, got_k, mine_k, stage):
        mine_k[...] = jnp.sum(hat * hat, axis=0, keepdims=True)
        share_k(lambda to: mine_k, got_k, stage)

    def scale_of(got_k, mine_k, got_p, mine_p, stage):
        mine_p[...] = total(mine_k[...], got_k, stage)
        share_plane(mine_p, got_p, stage + 1)
        return jnp.sqrt(total(mine_p[...], got_p, stage + 1) / total_rows + EPS)

    def make_inner(s):
        x_copy(s).wait()
        c_rows = c_slab[third[s]].astype(jnp.bfloat16)
        span = 8

        def one(n, carry):
            rows = x_buf[s, pl.ds(n * span, span)].reshape(span * edge, edge)
            value = jnp.dot(rows, c_rows, preferred_element_type=F32)
            inner[s, pl.ds(n * span, span)] = value.reshape(span, edge, rank)
            return carry

        lax.fori_loop(0, edge // span, one, 0)

    def x_copy(s):
        return pltpu.make_async_copy(x_hbm.at[s], x_buf.at[s], copy_sem.at[s])

    def position(stored, n_line):
        return (rem(stored, 2) * n_line + div(stored, n_k)) * n_z + div(rem(stored, n_k), 2)

    def load_rows(buf, coord, owner, n_line, s):
        for t in range(per_block):
            value = buf[position(owner[coord[s] * per_block + t], n_line)]
            rows_f32[s, pl.ds(t * piece, piece)] = value.astype(F32)

    def mode_one(s):
        def one(n, carry):
            span = 8
            for h in range(rank // HALF):
                lanes = pl.ds(h * HALF, HALF)
                value = inner[s, pl.ds(n * span, span), :, lanes]
                summed = jnp.sum(value * rows_f32[s, :, lanes][None], axis=1)
                contrib[s * per_block + div(n * span, piece), pl.ds(pl.multiple_of(rem(n * span, piece), span), span), lanes] = summed
            return carry

        lax.fori_loop(0, edge // 8, one, 0)

    def mode_two(s):
        def one(n, acc):
            for u in range(8):
                acc = acc + inner[s, n * 8 + u] * rows_f32[s, pl.ds(n * 8 + u, 1), :]
            return acc

        acc = lax.fori_loop(0, edge // 8, one, jnp.zeros((edge, rank), F32))
        contrib[pl.ds(s * per_block, per_block)] = acc.reshape(per_block, piece, rank)

    def find_spots(spots, coord, owner, n_line):
        count = owner.shape[0]
        none = 2 * per_block
        wanted = [[position(owner[coord[s] * per_block + t], n_line) for t in range(per_block)] for s in range(2)]
        live = [(s < filled[0]).astype(jnp.int32) for s in range(2)]

        def one(q, carry):
            for s in range(2):
                at = jnp.int32(none)
                for t in range(per_block):
                    hit = (wanted[s][t] == q).astype(jnp.int32)
                    at = at + hit * live[s] * (s * per_block + t - none)
                spots[s * count + q] = at
            return carry

        lax.fori_loop(0, count, one, 0)

    def place(spots, part, start):
        count = part.shape[0]

        def one(p, carry):
            q = start + rem(z + 1 + p, n_z)
            part[start + p] = contrib[spots[q]] + contrib[spots[count + q]]
            return carry

        lax.fori_loop(0, n_z, one, 0)

    for s in range(2):
        x_copy(s).start()
    gathered_b[(core * n_i + i) * n_z + z] = b_own[...].astype(jnp.bfloat16)
    barrier = pltpu.get_barrier_semaphore()

    def greet_k(d, carry):
        pl.semaphore_signal(barrier, inc=1, device_id={"ka": rem(k + d, n_k)}, device_id_type=MESH)
        return carry

    def greet_plane(d, carry):
        pl.semaphore_signal(barrier, inc=1, device_id=at_plane(rem(plane + d, n_plane)), device_id_type=MESH)
        return carry

    lax.fori_loop(1, n_k, greet_k, 0)
    lax.fori_loop(1, n_plane, greet_plane, 0)
    gram_chunks(b_own[...], local1, 0)
    gram_chunks(c_slab[div(plane, per_block), pl.ds(pl.multiple_of(rem(plane, per_block) * piece, piece), piece)], local1, 1)
    pl.semaphore_wait(barrier, n_k + n_plane - 2)

    gather_z(gathered_b, i, n_i, 0)
    share_k(lambda to: local1.at[to], gram1, 3)
    find_spots(spots_one, first, owner_one, n_j)
    find_spots(spots_two, second, owner_two, n_i)
    contrib[2 * per_block] = jnp.zeros((piece, rank), F32)
    arrived(gathered_b.at[pl.ds(0, n_z - 1)], 0)
    gather_line(gathered_b, "ia", i, n_i, 1, 22)
    make_inner(0)
    gather_core(gathered_b, i, n_i, 1, 22)
    make_inner(1)
    arrived(gathered_b.at[pl.ds(0, n_i * n_z)], 1)
    load_rows(gathered_b, second, owner_two, n_i, 0)
    mode_one(0)
    own1[...] = total(local1[k], gram1, 3)
    share_plane(own1, mix1, 4)
    load_rows(gathered_b, second, owner_two, n_i, 1)
    mode_one(1)
    scatter_core(part1, core1, spots_one, j, n_j, extra)
    grams = total(own1[...], mix1, 4)
    gram_c_own[...] = grams[1]
    gather_gram(full1, grams[0] * grams[1], 5)
    scatter_line(part1, core1, line1, "ja", j, n_j, extra, extra + n_j)
    arrived(full1.at[pl.ds(0, n_k - 1)], 5)
    invert_first(full1)
    scatter_z(part1, line1, zed1, j, n_j, extra + n_j, 8)
    invert_second()
    a_hat = solve(scatter_end(part1, zed1, j, n_j, 8))
    squares_start(a_hat, sq_ka.at[0], sq_kb.at[0], 9)
    hats[z] = a_hat

    def send_hat(d, carry):
        send(hats.at[z], hats.at[z], {"ka": rem(z + d, n_z) * 2 + core}, 11)
        return carry

    lax.fori_loop(1, n_z, send_hat, 0)
    sent((hats.at[pl.ds(0, n_z - 1)], 11))
    scale_a = scale_of(sq_ka.at[0], sq_kb.at[0], sq_la.at[0], sq_lb.at[0], 9)
    a_rows = a_hat / scale_a
    a_out[...] = a_rows

    arrived(hats.at[pl.ds(0, n_z - 1)], 11)

    def to_half(p, carry):
        gathered_a[(core * n_j + j) * n_z + p] = (hats[p] / scale_a).astype(jnp.bfloat16)
        return carry

    lax.fori_loop(0, n_z, to_half, 0)
    gather_line(gathered_a, "ja", j, n_j, 12, 22 + n_i)
    gram_chunks(a_rows, local2, 0)
    share_k(lambda to: local2.at[to], gram2, 14)
    gather_core(gathered_a, j, n_j, 12, 22 + n_i)
    own2[...] = total(local2[k], gram2, 14)
    share_plane(own2, mix2, 15)
    arrived(gathered_a.at[pl.ds(0, n_j * n_z)], 12)
    for s in range(2):
        load_rows(gathered_a, first, owner_one, n_j, s)
        mode_two(s)
    scatter_core(part2, core2, spots_two, i, n_i, extra2)
    gather_gram(full2, total(own2[...], mix2, 15)[0] * gram_c_own[...], 16)
    scatter_line(part2, core2, line2, "ia", i, n_i, extra2, extra2 + n_i)
    arrived(full2.at[pl.ds(0, n_k - 1)], 16)
    invert_first(full2)
    scatter_z(part2, line2, zed2, i, n_i, extra2 + n_i, 19)
    invert_second()
    b_hat = solve(scatter_end(part2, zed2, i, n_i, 19))
    squares_start(b_hat, sq_ka.at[1], sq_kb.at[1], 20)
    b_out[...] = b_hat / scale_of(sq_ka.at[1], sq_kb.at[1], sq_la.at[1], sq_lb.at[1], 20)

    for like, stage in sends:
        pltpu.make_async_copy(like, like, send_sem.at[stage]).wait()


def solution(mesh):
    n_i, n_j, n_k = (mesh.shape[name] for name in ("ia", "ja", "ka"))
    n_z = n_k // 2
    sizes = (n_i, n_j, n_k)

    def body(blocks, first, second, third, filled, owner_one, owner_two, factor_b, factor_c):
        piece, rank = factor_b.shape[1:]
        edge = blocks.shape[-1]
        chunk = rank // n_k
        n_plane = n_i * n_j
        stages = 22 + 2 * (n_i + n_j) + n_z // 2 * 2

        def vmem(*shape, dtype=F32):
            return pltpu.VMEM(shape, dtype)

        def scatter_buffers(n_line):
            return [
                vmem(2 * n_line * n_z, piece, rank),
                vmem(n_line * n_z, piece, rank),
                vmem(n_z // 2, n_line - 1, 2, piece, rank),
                vmem(n_z - 1, piece, rank),
            ]

        def gram_buffers(count):
            return [
                vmem(n_k, count, chunk, rank),
                vmem(n_k - 1, count, chunk, rank),
                vmem(n_plane - 1, count, chunk, rank),
                vmem(n_k, chunk, rank),
            ]

        scratch = [
            vmem(2, edge, edge, edge, dtype=jnp.bfloat16),
            vmem(2, edge, edge, rank),
            vmem(2 * n_i * n_z, piece, rank, dtype=jnp.bfloat16),
            vmem(2 * n_j * n_z, piece, rank, dtype=jnp.bfloat16),
            vmem(2, edge, rank),
            vmem(2 * edge // piece + 1, piece, rank),
            *scatter_buffers(n_j),
            *scatter_buffers(n_i),
            *gram_buffers(2),
            *gram_buffers(1),
            vmem(2, chunk, rank),
            vmem(1, chunk, rank),
            vmem(chunk, rank),
            vmem(2, n_k - 1, 1, rank),
            vmem(2, 1, rank),
            vmem(2, n_plane - 1, 1, rank),
            vmem(2, 1, rank),
            vmem(n_z, piece, rank),
            vmem(3, HALF, HALF),
            pltpu.SMEM((2 * owner_one.shape[0],), jnp.int32),
            pltpu.SMEM((2 * owner_two.shape[0],), jnp.int32),
            pltpu.SemaphoreType.DMA((2,)),
            pltpu.SemaphoreType.DMA((stages,)),
            pltpu.SemaphoreType.DMA((stages,)),
        ]
        smem = pl.BlockSpec(memory_space=pltpu.SMEM)
        whole = pl.BlockSpec(memory_space=pltpu.VMEM)
        a_own, b_own = pl.pallas_call(
            functools.partial(kernel, sizes),
            out_shape=[jax.ShapeDtypeStruct((piece, rank), F32)] * 2,
            in_specs=[smem] * 6 + [pl.BlockSpec(memory_space=pl.ANY), whole, whole],
            out_specs=[whole, whole],
            scratch_shapes=scratch,
            compiler_params=pltpu.CompilerParams(
                collective_id=0, has_side_effects=True, vmem_limit_bytes=62 * 1024 * 1024
            ),
            name="sweep",
        )(
            filled.reshape(1),
            first.reshape(2),
            second.reshape(2),
            third.reshape(2),
            owner_one,
            owner_two,
            blocks.reshape(blocks.shape[3:]),
            factor_b[0],
            factor_c[0].reshape(-1, edge, rank),
        )
        return a_own[None], b_own[None]

    return jax.shard_map(
        body,
        mesh=mesh,
        in_specs=(
            P("ia", "ja", "ka", None, None, None, None),
            P("ia", "ja", "ka", None),
            P("ia", "ja", "ka", None),
            P("ia", "ja", "ka", None),
            P("ia", "ja", "ka"),
            P(),
            P(),
            P("ja", ("ia", "ka"), None),
            P("ka", None, None),
        ),
        out_specs=(P("ia", ("ja", "ka"), None), P("ja", ("ia", "ka"), None)),
        check_vma=False,
    )
```

```python
import functools

import jax
import jax.numpy as jnp
from jax import lax
from jax.experimental import pallas as pl
from jax.experimental.pallas import tpu as pltpu
from jax.sharding import PartitionSpec as P

EPS = 1e-06
HALF = 128
GROUP = 8
MESH = pl.DeviceIdType.MESH
F32 = jnp.float32


def rem(a, b):
    return lax.rem(a, jnp.int32(b))


def div(a, b):
    return lax.div(a, jnp.int32(b))


def each(count, one):
    for d in range(1, count):
        one(d, 0)


def dot(a, b):
    return jnp.dot(a, b, precision=lax.Precision.HIGHEST, preferred_element_type=F32)


def dot_nt(a, b):
    return lax.dot_general(
        a, b, (((1,), (1,)), ((), ())), precision=lax.Precision.HIGHEST, preferred_element_type=F32
    )


def inverse_half(mat, start=0, stop=HALF // GROUP):
    lane = lax.broadcasted_iota(jnp.int32, (GROUP, HALF), 1)
    sub = lax.broadcasted_iota(jnp.int32, (GROUP, HALF), 0)
    lane_rest = lax.broadcasted_iota(jnp.int32, (HALF - GROUP, HALF), 1)

    def step(_, mat):
        top, rest = mat[:GROUP], mat[GROUP:]
        spread = [jnp.broadcast_to(top[:, t : t + 1], (GROUP, HALF)) for t in range(GROUP)]
        for s in range(GROUP):
            column = spread[s]
            inv = 1.0 / column[s : s + 1]
            row = jnp.where(lane[:1] == s, 1.0, top[s : s + 1]) * inv
            top = jnp.where(sub == s, row, jnp.where(lane == s, 0.0, top) - column * row)
            for t in range(s + 1, GROUP):
                entry = spread[t][s : s + 1] * inv
                spread[t] = jnp.where(sub == s, entry, spread[t] - column * entry)
        out = jnp.where(lane_rest < GROUP, 0.0, rest)
        for s in range(GROUP):
            out = out - rest[:, s : s + 1] * top[s : s + 1]
        return pltpu.roll(jnp.concatenate([out, top], axis=0), HALF - GROUP, 1)

    return lax.fori_loop(start, stop, step, mat)


def kernel(
    sizes,
    filled,
    first,
    second,
    third,
    owner_one,
    owner_two,
    x_hbm,
    b_own,
    c_slab,
    a_out,
    b_out,
    x_buf,
    inner,
    gathered_b,
    gathered_a,
    rows_f32,
    contrib,
    part1,
    core1,
    line1,
    zed1,
    part2,
    core2,
    line2,
    zed2,
    local1,
    gram1,
    mix1,
    full1,
    local2,
    gram2,
    mix2,
    full2,
    own1,
    own2,
    gram_c_own,
    sq_ka,
    sq_kb,
    sq_la,
    sq_lb,
    hats,
    factor,
    spots_one,
    spots_two,
    copy_sem,
    send_sem,
    recv_sem,
):
    n_i, n_j, n_k = sizes
    n_z = n_k // 2
    piece, rank = b_own.shape
    edge = x_hbm.shape[-1]
    per_block = edge // piece
    total_rows = n_i * n_j * n_k * piece
    chunk = rank // n_k
    i, j, k = lax.axis_index("ia"), lax.axis_index("ja"), lax.axis_index("ka")
    core = rem(k, 2)
    z = div(k, 2)
    plane = i * n_j + j
    n_plane = n_i * n_j
    sends = []
    extra = 22 + n_i + n_j
    extra2 = extra + n_j + n_z // 2

    def sent(pair):
        sends.append(pair)

    def send(src, dst, where, stage):
        pltpu.make_async_remote_copy(
            src_ref=src,
            dst_ref=dst,
            send_sem=send_sem.at[stage],
            recv_sem=recv_sem.at[stage],
            device_id=where,
            device_id_type=MESH,
        ).start()

    def arrived(like, stage):
        pltpu.make_async_copy(like, like, recv_sem.at[stage]).wait()

    def at_plane(g):
        return {"ia": div(g, n_j), "ja": rem(g, n_j)}

    def gather_z(buf, line, n_line, stage):
        mine = buf.at[(core * n_line + line) * n_z + z]

        def one(d, carry):
            send(mine, mine, {"ka": rem(z + d, n_z) * 2 + core}, stage)
            return carry

        each(n_z, one)
        sent((buf.at[pl.ds(0, n_z - 1)], stage))

    def gather_line(buf, axis, line, n_line, stage, lines):
        mine = buf.at[pl.ds((core * n_line + line) * n_z, n_z)]
        for d in range(1, n_line):
            send(mine, mine, {axis: rem(line + d, n_line)}, lines + d)
            sent((buf.at[pl.ds(0, n_z)], lines + d))
        send(mine, mine, {"ka": z * 2 + 1 - core}, stage)

    def gather_core(buf, line, n_line, stage, lines):
        for d in sorted(range(1, n_line), key=lambda d: min(d, n_line - d)):
            arrived(buf.at[pl.ds(0, n_z)], lines + d)
            mine = buf.at[pl.ds((core * n_line + rem(line + n_line - d, n_line)) * n_z, n_z)]
            send(mine, mine, {"ka": z * 2 + 1 - core}, stage)
        sent((buf.at[pl.ds(0, n_line * n_z)], stage))

    pair = 2

    def scatter_core(part, got, spots, line, n_line, stage):
        for d in [*range(1, n_line), 0]:
            at = rem(line + d, n_line) * n_z
            far = (1 - core) * n_line * n_z + at
            place(spots, part, far)
            send(part.at[pl.ds(far, n_z)], got.at[pl.ds(at, n_z)], {"ka": z * 2 + 1 - core}, stage + d)
            sent((got.at[pl.ds(0, n_z)], stage + d))
        for d in range(n_line):
            place(spots, part, (core * n_line + rem(line + d, n_line)) * n_z)

    def add_core(part, got_core, line, n_line, d, stage):
        at = rem(line + d, n_line) * n_z
        arrived(got_core.at[pl.ds(0, n_z)], stage + d)
        mine = pl.ds(core * n_line * n_z + at, n_z)
        part[mine] = part[mine] + got_core[pl.ds(at, n_z)]

    def scatter_line(part, got_core, got, axis, line, n_line, core_stage, stage):
        for d in range(1, n_line):
            add_core(part, got_core, line, n_line, d, core_stage)
            to = rem(line + d, n_line)
            base = (core * n_line + to) * n_z
            for g in range(n_z // pair):
                send(part.at[pl.ds(base + g * pair, pair)], got.at[g, d - 1], {axis: to}, stage + g)
        for g in range(n_z // pair):
            sent((got.at[g], stage + g))
        add_core(part, got_core, line, n_line, 0, core_stage)

    def scatter_z(part, got_line, got, line, n_line, line_stage, stage, groups):
        base = (core * n_line + line) * n_z
        for g in groups:
            arrived(got_line.at[g], line_stage + g)
            group = pl.ds(base + g * pair, pair)
            value = part[group]
            for d in range(n_line - 1):
                value = value + got_line[g, d]
            part[group] = value
            for p in range(g * pair, (g + 1) * pair):
                if p < n_z - 1:
                    send(part.at[base + p], got.at[p], {"ka": rem(z + p + 1, n_z) * 2 + core}, stage)
        if n_z // pair - 1 in groups:
            sent((got, stage))

    def scatter_end(part, got, line, n_line, stage):
        arrived(got, stage)
        value = part[(core * n_line + line) * n_z + n_z - 1]
        for d in range(n_z - 1):
            value = value + got[d]
        return value

    def share_k(source, got, stage):
        def one(d, carry):
            send(source(rem(k + d, n_k)), got.at[d - 1], {"ka": rem(k + d, n_k)}, stage)
            return carry

        each(n_k, one)
        sent((got, stage))

    def share_plane(source, got, stage):
        def one(d, carry):
            send(source, got.at[d - 1], at_plane(rem(plane + d, n_plane)), stage)
            return carry

        each(n_plane, one)
        sent((got, stage))

    def total(value, got, stage):
        arrived(got, stage)
        return lax.fori_loop(0, got.shape[0], lambda d, acc: acc + got[d], value)

    def gram_chunks(rows, local, which):
        value = dot(rows.T, rows)
        local[:, which] = value.reshape(n_k, chunk, rank)

    def gather_gram(full, value, stage):
        full[k] = value

        def one(d, carry):
            send(full.at[k], full.at[k], {"ka": rem(k + d, n_k)}, stage)
            return carry

        each(n_k, one)
        sent((full.at[pl.ds(0, n_k - 1)], stage))

    def invert_first(full, between):
        mat = full[...].reshape(rank, rank)
        middle = HALF // GROUP // 2
        factor[0] = inverse_half(mat[:HALF, :HALF], 0, middle)
        between()
        pinv = inverse_half(factor[0], middle)
        cross = full[...].reshape(rank, rank)[:HALF, HALF:]
        w = dot(pinv, cross)
        factor[0] = pinv
        factor[1] = w
        factor[2] = full[...].reshape(rank, rank)[HALF:, HALF:] - dot(cross.T, w)

    def invert_second():
        factor[2] = inverse_half(factor[2])

    def solve(rows):
        left, right = rows[:, :HALF], rows[:, HALF:]
        w = factor[1]
        v = dot(dot(left, w) - right, factor[2])
        return jnp.concatenate([dot(left, factor[0]) + dot_nt(v, w), -v], axis=1)

    def squares_start(hat, got_k, mine_k, stage):
        mine_k[...] = jnp.sum(hat * hat, axis=0, keepdims=True)
        share_k(lambda to: mine_k, got_k, stage)

    def scale_of(got_k, mine_k, got_p, mine_p, stage):
        mine_p[...] = total(mine_k[...], got_k, stage)
        share_plane(mine_p, got_p, stage + 1)
        return jnp.sqrt(total(mine_p[...], got_p, stage + 1) / total_rows + EPS)

    def make_inner(s):
        x_copy(s).wait()
        c_rows = c_slab[third[s]].astype(jnp.bfloat16)
        span = 8

        def one(n, carry):
            rows = x_buf[s, pl.ds(n * span, span)].reshape(span * edge, edge)
            value = jnp.dot(rows, c_rows, preferred_element_type=F32)
            inner[s, pl.ds(n * span, span)] = value.reshape(span, edge, rank)
            return carry

        lax.fori_loop(0, edge // span, one, 0)

    def x_copy(s):
        return pltpu.make_async_copy(x_hbm.at[s], x_buf.at[s], copy_sem.at[s])

    def position(stored, n_line):
        return (rem(stored, 2) * n_line + div(stored, n_k)) * n_z + div(rem(stored, n_k), 2)

    def load_rows(buf, coord, owner, n_line, s):
        for t in range(per_block):
            value = buf[position(owner[coord[s] * per_block + t], n_line)]
            rows_f32[s, pl.ds(t * piece, piece)] = value.astype(F32)

    def mode_one(s):
        def one(n, carry):
            span = 8
            for h in range(rank // HALF):
                lanes = pl.ds(h * HALF, HALF)
                value = inner[s, pl.ds(n * span, span), :, lanes]
                summed = jnp.sum(value * rows_f32[s, :, lanes][None], axis=1)
                contrib[s * per_block + div(n * span, piece), pl.ds(pl.multiple_of(rem(n * span, piece), span), span), lanes] = summed
            return carry

        lax.fori_loop(0, edge // 8, one, 0)

    def mode_two(s):
        def one(n, acc):
            for u in range(8):
                acc = acc + inner[s, n * 8 + u] * rows_f32[s, pl.ds(n * 8 + u, 1), :]
            return acc

        acc = lax.fori_loop(0, edge // 8, one, jnp.zeros((edge, rank), F32))
        contrib[pl.ds(s * per_block, per_block)] = acc.reshape(per_block, piece, rank)

    def find_spots(spots, coord, owner, n_line):
        count = owner.shape[0]
        none = 2 * per_block
        wanted = [[position(owner[coord[s] * per_block + t], n_line) for t in range(per_block)] for s in range(2)]
        live = [(s < filled[0]).astype(jnp.int32) for s in range(2)]

        def one(q, carry):
            for s in range(2):
                at = jnp.int32(none)
                for t in range(per_block):
                    hit = (wanted[s][t] == q).astype(jnp.int32)
                    at = at + hit * live[s] * (s * per_block + t - none)
                spots[s * count + q] = at
            return carry

        lax.fori_loop(0, count, one, 0)

    def place(spots, part, start):
        count = part.shape[0]

        def one(p, carry):
            q = start + rem(z + 1 + p, n_z)
            part[start + p] = contrib[spots[q]] + contrib[spots[count + q]]
            return carry

        lax.fori_loop(0, n_z, one, 0)

    for s in range(2):
        x_copy(s).start()
    gathered_b[(core * n_i + i) * n_z + z] = b_own[...].astype(jnp.bfloat16)
    barrier = pltpu.get_barrier_semaphore()

    def greet_k(d, carry):
        pl.semaphore_signal(barrier, inc=1, device_id={"ka": rem(k + d, n_k)}, device_id_type=MESH)
        return carry

    def greet_plane(d, carry):
        pl.semaphore_signal(barrier, inc=1, device_id=at_plane(rem(plane + d, n_plane)), device_id_type=MESH)
        return carry

    lax.fori_loop(1, n_k, greet_k, 0)
    lax.fori_loop(1, n_plane, greet_plane, 0)
    gram_chunks(b_own[...], local1, 0)
    gram_chunks(c_slab[...].reshape(-1, rank), local1, 1)
    pl.semaphore_wait(barrier, n_k + n_plane - 2)

    gather_z(gathered_b, i, n_i, 0)
    share_k(lambda to: local1.at[to], gram1, 3)
    find_spots(spots_one, first, owner_one, n_j)
    find_spots(spots_two, second, owner_two, n_i)
    contrib[2 * per_block] = jnp.zeros((piece, rank), F32)
    arrived(gathered_b.at[pl.ds(0, n_z - 1)], 0)
    gather_line(gathered_b, "ia", i, n_i, 1, 22)
    make_inner(0)
    gather_core(gathered_b, i, n_i, 1, 22)
    make_inner(1)
    arrived(gathered_b.at[pl.ds(0, n_i * n_z)], 1)
    load_rows(gathered_b, second, owner_two, n_i, 0)
    mode_one(0)
    grams = total(local1[k], gram1, 3)
    own1[...] = grams[:1]
    gram_c_own[...] = grams[1]
    share_plane(own1, mix1, 4)
    load_rows(gathered_b, second, owner_two, n_i, 1)
    mode_one(1)
    scatter_core(part1, core1, spots_one, j, n_j, extra)
    gather_gram(full1, total(own1[...], mix1, 4)[0] * gram_c_own[...], 5)
    scatter_line(part1, core1, line1, "ja", j, n_j, extra, extra + n_j)
    groups = list(range(n_z // pair))
    on_one = functools.partial(scatter_z, part1, line1, zed1, j, n_j, extra + n_j, 8)
    on_one(groups[:-2])
    arrived(full1.at[pl.ds(0, n_k - 1)], 5)
    invert_first(full1, lambda: on_one(groups[-2:-1]))
    on_one(groups[-1:])
    invert_second()
    a_hat = solve(scatter_end(part1, zed1, j, n_j, 8))
    squares_start(a_hat, sq_ka.at[0], sq_kb.at[0], 9)
    hats[z] = a_hat

    def send_hat(d, carry):
        send(hats.at[z], hats.at[z], {"ka": rem(z + d, n_z) * 2 + core}, 11)
        return carry

    each(n_z, send_hat)
    sent((hats.at[pl.ds(0, n_z - 1)], 11))
    scale_a = scale_of(sq_ka.at[0], sq_kb.at[0], sq_la.at[0], sq_lb.at[0], 9)
    a_rows = a_hat / scale_a
    a_out[...] = a_rows

    arrived(hats.at[pl.ds(0, n_z - 1)], 11)

    def to_half(p, carry):
        gathered_a[(core * n_j + j) * n_z + p] = (hats[p] / scale_a).astype(jnp.bfloat16)
        return carry

    lax.fori_loop(0, n_z, to_half, 0)
    gather_line(gathered_a, "ja", j, n_j, 12, 22 + n_i)
    gram_chunks(a_rows, local2, 0)
    share_k(lambda to: local2.at[to], gram2, 14)
    gather_core(gathered_a, j, n_j, 12, 22 + n_i)
    own2[...] = total(local2[k], gram2, 14)
    share_plane(own2, mix2, 15)
    arrived(gathered_a.at[pl.ds(0, n_j * n_z)], 12)
    for s in range(2):
        load_rows(gathered_a, first, owner_one, n_j, s)
        mode_two(s)
    scatter_core(part2, core2, spots_two, i, n_i, extra2)
    gather_gram(full2, total(own2[...], mix2, 15)[0] * gram_c_own[...], 16)
    scatter_line(part2, core2, line2, "ia", i, n_i, extra2, extra2 + n_i)
    on_two = functools.partial(scatter_z, part2, line2, zed2, i, n_i, extra2 + n_i, 19)
    on_two(groups[:-2])
    arrived(full2.at[pl.ds(0, n_k - 1)], 16)
    invert_first(full2, lambda: on_two(groups[-2:-1]))
    on_two(groups[-1:])
    invert_second()
    b_hat = solve(scatter_end(part2, zed2, i, n_i, 19))
    squares_start(b_hat, sq_ka.at[1], sq_kb.at[1], 20)
    b_out[...] = b_hat / scale_of(sq_ka.at[1], sq_kb.at[1], sq_la.at[1], sq_lb.at[1], 20)

    for like, stage in sends:
        pltpu.make_async_copy(like, like, send_sem.at[stage]).wait()


def solution(mesh):
    n_i, n_j, n_k = (mesh.shape[name] for name in ("ia", "ja", "ka"))
    n_z = n_k // 2
    sizes = (n_i, n_j, n_k)

    def body(blocks, first, second, third, filled, owner_one, owner_two, factor_b, factor_c):
        piece, rank = factor_b.shape[1:]
        edge = blocks.shape[-1]
        chunk = rank // n_k
        n_plane = n_i * n_j
        stages = 22 + 2 * (n_i + n_j) + n_z // 2 * 2

        def vmem(*shape, dtype=F32):
            return pltpu.VMEM(shape, dtype)

        def scatter_buffers(n_line):
            return [
                vmem(2 * n_line * n_z, piece, rank),
                vmem(n_line * n_z, piece, rank),
                vmem(n_z // 2, n_line - 1, 2, piece, rank),
                vmem(n_z - 1, piece, rank),
            ]

        def gram_buffers(count):
            return [
                vmem(n_k, count, chunk, rank),
                vmem(n_k - 1, count, chunk, rank),
                vmem(n_plane - 1, 1, chunk, rank),
                vmem(n_k, chunk, rank),
            ]

        scratch = [
            vmem(2, edge, edge, edge, dtype=jnp.bfloat16),
            vmem(2, edge, edge, rank),
            vmem(2 * n_i * n_z, piece, rank, dtype=jnp.bfloat16),
            vmem(2 * n_j * n_z, piece, rank, dtype=jnp.bfloat16),
            vmem(2, edge, rank),
            vmem(2 * edge // piece + 1, piece, rank),
            *scatter_buffers(n_j),
            *scatter_buffers(n_i),
            *gram_buffers(2),
            *gram_buffers(1),
            vmem(1, chunk, rank),
            vmem(1, chunk, rank),
            vmem(chunk, rank),
            vmem(2, n_k - 1, 1, rank),
            vmem(2, 1, rank),
            vmem(2, n_plane - 1, 1, rank),
            vmem(2, 1, rank),
            vmem(n_z, piece, rank),
            vmem(3, HALF, HALF),
            pltpu.SMEM((2 * owner_one.shape[0],), jnp.int32),
            pltpu.SMEM((2 * owner_two.shape[0],), jnp.int32),
            pltpu.SemaphoreType.DMA((2,)),
            pltpu.SemaphoreType.DMA((stages,)),
            pltpu.SemaphoreType.DMA((stages,)),
        ]
        smem = pl.BlockSpec(memory_space=pltpu.SMEM)
        whole = pl.BlockSpec(memory_space=pltpu.VMEM)
        a_own, b_own = pl.pallas_call(
            functools.partial(kernel, sizes),
            out_shape=[jax.ShapeDtypeStruct((piece, rank), F32)] * 2,
            in_specs=[smem] * 6 + [pl.BlockSpec(memory_space=pl.ANY), whole, whole],
            out_specs=[whole, whole],
            scratch_shapes=scratch,
            compiler_params=pltpu.CompilerParams(
                collective_id=0, has_side_effects=True, vmem_limit_bytes=62 * 1024 * 1024
            ),
            name="sweep",
        )(
            filled.reshape(1),
            first.reshape(2),
            second.reshape(2),
            third.reshape(2),
            owner_one,
            owner_two,
            blocks.reshape(blocks.shape[3:]),
            factor_b[0],
            factor_c[0].reshape(-1, edge, rank),
        )
        return a_own[None], b_own[None]

    return jax.shard_map(
        body,
        mesh=mesh,
        in_specs=(
            P("ia", "ja", "ka", None, None, None, None),
            P("ia", "ja", "ka", None),
            P("ia", "ja", "ka", None),
            P("ia", "ja", "ka", None),
            P("ia", "ja", "ka"),
            P(),
            P(),
            P("ja", ("ia", "ka"), None),
            P("ka", None, None),
        ),
        out_specs=(P("ia", ("ja", "ka"), None), P("ja", ("ia", "ka"), None)),
        check_vma=False,
    )
```
